512 devices in a mesh: nodes: 128 (over x_lo, y, z), cols: 4 (over x_hi, core).
Axes of the slice: x: 4 (x_hi: 2, x_lo: 2; x = x_hi * 2 + x_lo), y: 4, z: 16, core: 2. Of those that a mesh axis runs over, the one named last changes fastest.
Arguments:
- vectors: bfloat16 [512, 4, 6, 16, 512], P('nodes', None, None, None, 'cols'), may hold values from -6 to 6
- node_shift: bfloat16 [512, 6, 16], P('nodes'), may hold values from 0.5 to 2
- coupling: float32 [4, 4], replicated, may hold values from -3 to 3
- dual_basis: bfloat16 [196608, 512], P(('nodes', 'cols')), may hold values from -0.013671875 to 0.013671875
Outputs:
- gram_matrix: float32 [512, 512], P('cols')
- rotated: bfloat16 [196608, 512], P(('nodes', 'cols'))
The draws below stay inside these ranges and needn't reach their ends.
All inputs are finite; a program needn't handle non-finite values.
Results may differ from the reference program's by a relative error of at most 0.0064.
Values may be sent and summed in bfloat16 or wider, within the bound.
No kernel may reach another device: no remote copies, remote signals or barrier semaphores. Data moves between devices by JAX's collectives and lax.ppermute only.
A program may use at most 64 MiB of HBM per device.

```python
import math
import jax
import jax.numpy as jnp
from jax import lax

VECS = 512
DOFS = 4
GY = 6
GZ = 16
NX = 512
ROWS = 196608


def levels(stream_key, shape, pieces, least, high):
    gain, own = 1.0, jax.random.fold_in(stream_key, 6)
    for axis_at, blocks in pieces:
        heights = jnp.exp(jax.random.uniform(jax.random.fold_in(own, axis_at), (blocks,), jnp.float32, least / len(pieces), high / len(pieces)))
        gain = gain * jnp.repeat(heights, shape[axis_at] // blocks).reshape([-1 if axis == axis_at else 1 for axis in range(len(shape))])
    return gain


def bell_draw(rng, extent, width, reach, shards=(), dtype=jnp.bfloat16):
    entries = jax.random.normal(rng, extent, jnp.float32) * width
    if len(shards) > 0:
        entries = levels(rng, extent, shards, -0.22, 0.18) * entries
    return jnp.clip(entries, min=-reach, max=reach).astype(dtype)


def setup_inputs(seed: int = 0) -> dict:
    splits = jax.random.split(jax.random.key(seed), 5)
    return {
        "vectors": bell_draw(splits[0], (NX, DOFS, GY, GZ, VECS), 1.0, 6.0, ((0, 128), (4, 4))),
        "node_shift": jnp.clip(0.5 + 1.5 * jax.random.uniform(splits[1], (NX, GY, GZ), jnp.float32) ** levels(splits[1], (NX, GY, GZ), ((0, 128),), -0.2, 0.2), 0.5, 2.0).astype(jnp.bfloat16),
        "coupling": bell_draw(splits[2], (DOFS, DOFS), 1.0, 3.0, (), jnp.float32),
        "dual_basis": bell_draw(splits[3], (ROWS, VECS), ROWS ** -0.5, 0.013671875, ((0, 512),)),
    }


center_value = 10.0
half_width = 7.0


def operate(field_in, shift_full, coupling):
    padded = jnp.pad(field_in, ((1, 1), (0, 0), (1, 1), (1, 1), (0, 0)))
    beside = padded[2:, :, 1:-1, 1:-1] + padded[:-2, :, 1:-1, 1:-1]
    beside = beside + padded[1:-1, :, 2:, 1:-1] + padded[1:-1, :, :-2, 1:-1]
    beside = beside + padded[1:-1, :, 1:-1, 2:] + padded[1:-1, :, 1:-1, :-2]
    coupled = jnp.einsum('de,xeyzc->xdyzc', coupling, field_in, precision=lax.Precision.HIGHEST)
    return (6.0 + shift_full[:, None, :, :, None]) * field_in - beside + coupled


def reference(vectors, node_shift, coupling, dual_basis):
    shift_full = node_shift.astype(jnp.float32)
    block_width = math.gcd(VECS, 64)
    count_blocks = VECS // block_width
    split_cols = vectors.reshape(NX, DOFS, GY, GZ, count_blocks, block_width)
    split_cols = jnp.moveaxis(split_cols, 4, 0)

    def filter_block(col_block):
        state_zero = col_block.astype(jnp.float32)
        state_one = (operate(state_zero, shift_full, coupling) - center_value * state_zero) / half_width
        state_two = 2.0 * (operate(state_one, shift_full, coupling) - center_value * state_one) / half_width - state_zero
        state_three = 2.0 * (operate(state_two, shift_full, coupling) - center_value * state_two) / half_width - state_one
        return state_three.astype(jnp.bfloat16)

    filtered = lax.map(filter_block, split_cols)
    filtered = jnp.moveaxis(filtered, 0, 4).reshape(ROWS, VECS)
    gram_matrix = lax.dot_general(dual_basis, filtered, (((0,), (0,)), ((), ())), preferred_element_type=jnp.float32)
    gram_half = gram_matrix.astype(jnp.bfloat16)
    rotated = jnp.dot(filtered, gram_half, preferred_element_type=jnp.float32) * (VECS ** -0.5)
    return gram_matrix, rotated.astype(jnp.bfloat16)
```

```python
import functools

import jax
import jax.numpy as jnp
from jax import lax
from jax.experimental import pallas as pl
from jax.experimental.pallas import tpu as pltpu
from jax.sharding import Mesh
from jax.sharding import PartitionSpec as P

NODES = ("x_lo", "y", "z_hi", "z_lo")
COLS = ("x_hi", "core")
NEAR = ("x_lo", "y", "z_lo", "x_hi", "core")
FAR = "z_hi"
REACH = 3
TILE_ROWS = 16
LANES = 128

bf16 = jnp.bfloat16
f32 = jnp.float32


def vmem(count):
    return [pl.BlockSpec(memory_space=pltpu.VMEM)] * count


def smem(count):
    return [pl.BlockSpec(memory_space=pltpu.SMEM)] * count


def room(mebibytes):
    return pltpu.CompilerParams(vmem_limit_bytes=mebibytes << 20)


def pack_kernel(v_ref, shift_ref, up_ref, down_ref):
    layers, rows = v_ref.shape[0], v_ref.shape[1]
    for k in range(REACH):
        up_ref[k * rows : (k + 1) * rows, :] = v_ref[layers - REACH + k]
        down_ref[k * rows : (k + 1) * rows, :] = v_ref[k]
    up_ref[REACH * rows :, :] = shift_ref[...]
    down_ref[REACH * rows :, :] = shift_ref[...]


def filter_kernel(
    gy, dofs, coup_ref, place_ref, v_ref, low_ref, high_ref, shift_ref, out_ref, s0, s1, s2, diag
):
    layers = v_ref.shape[0]
    gz = TILE_ROWS
    rows = dofs * gy * gz
    tiles = dofs * gy
    low_in = place_ref[0].astype(f32)
    high_in = place_ref[1].astype(f32)

    def shift_cols(ref, first, layer, slot):
        tile = ref[first : first + gz, :].astype(f32)
        for y in range(gy):
            k = layer * gy + y
            diag[slot, y] = jnp.broadcast_to(tile[:, k : k + 1], (gz, LANES)) - 4.0

    for k in range(2):
        shift_cols(low_ref, REACH * rows, layers - 2 + k, k)
        shift_cols(high_ref, REACH * rows, k, 2 + layers + k)
    for k in range(layers):
        shift_cols(shift_ref, 0, k, 2 + k)

    for t in range(tiles):
        for k in range(REACH):
            at = k * rows + t * gz
            s0[k, t] = low_ref[at : at + gz, :].astype(f32)
            s0[REACH + layers + k, t] = high_ref[at : at + gz, :].astype(f32)
        for k in range(layers):
            s0[REACH + k, t] = v_ref[k, t * gz : (t + 1) * gz, :].astype(f32)

    row = lax.broadcasted_iota(jnp.int32, (gz, LANES), 0)
    top, bottom = row == 0, row == gz - 1
    coup = [[coup_ref[d, e] for e in range(dofs)] for d in range(dofs)]

    def apply(src, at, dslot, emit):
        for y in range(gy):
            mid = [src[at, d * gy + y] for d in range(dofs)]
            dg = diag[dslot, y]
            for d in range(dofs):
                t = d * gy + y
                near = src[at - 1, t] + src[at + 1, t]
                if y > 0:
                    near = near + src[at, t - 1]
                if y < gy - 1:
                    near = near + src[at, t + 1]
                near = near + jnp.where(top, 0.0, pltpu.roll(mid[d], 1, 0))
                near = near + jnp.where(bottom, 0.0, pltpu.roll(mid[d], gz - 1, 0))
                total = (dg + coup[d][d]) * mid[d] - near
                for e in range(dofs):
                    if e != d:
                        total = total + coup[d][e] * mid[e]
                emit(t, total)

    def outside(layer):
        keep = jnp.where(layer < 0, low_in, jnp.where(layer >= layers, high_in, 1.0))
        return keep

    @pl.loop(0, layers + 4)
    def _(i):
        keep = outside(i - 2)

        def emit(t, total):
            s1[i, t] = total * keep

        apply(s0, i + 1, i, emit)

    @pl.loop(0, layers + 2)
    def _(i):
        keep = outside(i - 1)

        def emit(t, total):
            s2[i, t] = (total - 24.5 * s0[i + 2, t]) * keep

        apply(s1, i + 1, i + 1, emit)

    @pl.loop(0, layers)
    def _(i):
        def emit(t, total):
            last = (total - 12.25 * s1[i + 2, t]) * (4.0 / 343.0)
            out_ref[i, t * gz : (t + 1) * gz, :] = last.astype(bf16)

        apply(s2, i + 1, i + 2, emit)


def side_by_side(parts):
    return jnp.concatenate(parts, axis=1)


def gram_kernel(dual_ref, f_ref, out_ref):
    blocks = f_ref.shape[0]
    pieces, height, _ = out_ref.shape
    each = pieces // blocks
    dual = dual_ref[...]
    for b in range(0, blocks, 2):
        pair = side_by_side([f_ref[b], f_ref[b + 1]])
        part = lax.dot_general(dual, pair, (((0,), (0,)), ((), ())), preferred_element_type=f32)
        for k in range(2):
            cut = part[:, k * LANES : (k + 1) * LANES].astype(bf16)
            out_ref[(b + k) * each : (b + k + 1) * each] = cut.reshape(each, height, LANES)


def sum_kernel(in_ref, out_ref):
    count = in_ref.shape[0]
    total = in_ref[0].astype(f32)
    for k in range(1, count):
        total = total + in_ref[k].astype(f32)
    piece = total.astype(bf16)
    for k in range(out_ref.shape[0]):
        out_ref[k] = piece


def rotate_kernel(scale, place_ref, f_ref, g_ref, gram_ref, out_ref):
    blocks, rows, _ = f_ref.shape
    pieces, height, _ = g_ref.shape
    each = pieces // blocks
    own = each // blocks
    cols = side_by_side([f_ref[b] for b in range(blocks)])
    first = place_ref[2] * own
    for b in range(0, blocks, 2):
        pair = side_by_side(
            [g_ref[k * each : (k + 1) * each].reshape(each * height, LANES) for k in (b, b + 1)]
        )
        turned = jnp.dot(cols, pair, preferred_element_type=f32) * scale
        out_ref[:, b * LANES : (b + 2) * LANES] = turned.astype(bf16)
        for k in (b, b + 1):
            mine = g_ref[pl.ds(k * each + first, own)].reshape(own * height, LANES)
            gram_ref[:, k * LANES : (k + 1) * LANES] = mine.astype(f32)


def shards(vectors, node_shift, coupling, dual_basis):
    layers, dofs, gy, gz, width = vectors.shape
    rows = dofs * gy * gz
    count = lax.axis_size(NODES)
    near = lax.axis_size(NEAR)
    far = lax.axis_size(FAR)
    blocks = lax.axis_size(COLS)
    cols = blocks * width
    height = cols * blocks // near
    v = vectors.reshape(layers, rows, width)
    shift_tile = jnp.pad(
        node_shift.transpose(2, 0, 1).reshape(gz, layers * gy), ((0, 0), (0, LANES - layers * gy))
    )
    message = jax.ShapeDtypeStruct((REACH * rows + gz, width), bf16)
    up, down = pl.pallas_call(
        pack_kernel, out_shape=(message, message), in_specs=vmem(2), out_specs=tuple(vmem(2)),
        compiler_params=room(8), name="pack",
    )(v, shift_tile)
    low = lax.ppermute(up, NODES, [(i, i + 1) for i in range(count - 1)])
    high = lax.ppermute(down, NODES, [(i + 1, i) for i in range(count - 1)])
    node = lax.axis_index(NODES)
    place = jnp.stack([node > 0, node < count - 1, lax.axis_index(COLS)]).astype(jnp.int32)
    tiles = dofs * gy
    own = pl.pallas_call(
        functools.partial(filter_kernel, gy, dofs),
        out_shape=jax.ShapeDtypeStruct((layers, rows, width), bf16),
        in_specs=smem(2) + vmem(4),
        out_specs=vmem(1)[0],
        scratch_shapes=[
            pltpu.VMEM((layers + 6, tiles, gz, width), f32),
            pltpu.VMEM((layers + 4, tiles, gz, width), f32),
            pltpu.VMEM((layers + 2, tiles, gz, width), f32),
            pltpu.VMEM((layers + 4, gy, gz, width), f32),
        ],
        compiler_params=room(16), name="filter",
    )(coupling, place, v, low, high, shift_tile)
    mine = lax.all_to_all(own, COLS, split_axis=0, concat_axis=0, tiled=True)
    terms = pl.pallas_call(
        gram_kernel,
        out_shape=jax.ShapeDtypeStruct((near, height, LANES), bf16),
        in_specs=vmem(2), out_specs=vmem(1)[0], compiler_params=room(8), name="gram",
    )(dual_basis, mine)

    def summed(pieces, copies, name):
        return pl.pallas_call(
            sum_kernel,
            out_shape=jax.ShapeDtypeStruct((copies, height, LANES), bf16),
            in_specs=vmem(1), out_specs=vmem(1)[0], compiler_params=room(8), name=name,
        )(pieces)

    pieces = lax.all_to_all(terms, NEAR, split_axis=0, concat_axis=0, tiled=True)
    pieces = lax.all_to_all(summed(pieces, far, "near_sum"), FAR, split_axis=0, concat_axis=0, tiled=True)
    pieces = lax.all_to_all(summed(pieces, near, "far_sum"), NEAR, split_axis=0, concat_axis=0, tiled=True)
    gram, rotated = pl.pallas_call(
        functools.partial(rotate_kernel, cols ** (-0.5)),
        out_shape=(
            jax.ShapeDtypeStruct((cols // blocks, cols), f32),
            jax.ShapeDtypeStruct((rows, cols), bf16),
        ),
        in_specs=smem(1) + vmem(2), out_specs=tuple(vmem(2)), compiler_params=room(12), name="rotate",
    )(place, mine, pieces)
    return gram, rotated


SIZES = (2, 4, 8, 2, 2, 2)


def solution(mesh):
    torus = Mesh(mesh.devices.reshape(SIZES), NODES + COLS)
    placed = (P(NODES, None, None, None, COLS), P(NODES, None, None), P(), P(NODES + COLS, None))
    return jax.shard_map(
        shards,
        mesh=torus,
        in_specs=placed,
        out_specs=(P(COLS, None), P(NODES + COLS, None)),
        check_vma=False,
    )
```

```python
import functools

import jax
import jax.numpy as jnp
from jax import lax
from jax.experimental import pallas as pl
from jax.experimental.pallas import tpu as pltpu
from jax.sharding import Mesh
from jax.sharding import PartitionSpec as P


NODES = ("x_lo", "y", "z_hi", "z_lo")
COLS = ("x_hi", "core")
NEAR = ("x_lo", "y", "z_lo", "core")
HALVES = "x_hi"
FAR = "z_hi"
REACH = 3
TILE_ROWS = 16
LANES = 128

bf16 = jnp.bfloat16
f32 = jnp.float32


def vmem(count):
    return [pl.BlockSpec(memory_space=pltpu.VMEM)] * count


def smem(count):
    return [pl.BlockSpec(memory_space=pltpu.SMEM)] * count


def room(mebibytes):
    return pltpu.CompilerParams(vmem_limit_bytes=mebibytes << 20)


def pack_kernel(v_ref, shift_ref, up_ref, down_ref):
    layers, rows = v_ref.shape[0], v_ref.shape[1]
    for k in range(REACH):
        up_ref[k * rows : (k + 1) * rows, :] = v_ref[layers - REACH + k]
        down_ref[k * rows : (k + 1) * rows, :] = v_ref[k]
    up_ref[REACH * rows :, :] = shift_ref[...]
    down_ref[REACH * rows :, :] = shift_ref[...]


def filter_kernel(
    gy, dofs, coup_ref, place_ref, v_ref, low_ref, high_ref, shift_ref, out_ref, s0, s1, s2, diag
):
    layers = v_ref.shape[0]
    gz = TILE_ROWS
    rows = dofs * gy * gz
    tiles = dofs * gy
    low_in = place_ref[0].astype(f32)
    high_in = place_ref[1].astype(f32)

    def shift_cols(ref, first, layer, slot):
        tile = ref[first : first + gz, :].astype(f32)
        for y in range(gy):
            k = layer * gy + y
            diag[slot, y] = jnp.broadcast_to(tile[:, k : k + 1], (gz, LANES)) - 4.0

    for k in range(2):
        shift_cols(low_ref, REACH * rows, layers - 2 + k, k)
        shift_cols(high_ref, REACH * rows, k, 2 + layers + k)
    for k in range(layers):
        shift_cols(shift_ref, 0, k, 2 + k)

    for t in range(tiles):
        for k in range(REACH):
            at = k * rows + t * gz
            s0[k, t] = low_ref[at : at + gz, :].astype(f32)
            s0[REACH + layers + k, t] = high_ref[at : at + gz, :].astype(f32)
        for k in range(layers):
            s0[REACH + k, t] = v_ref[k, t * gz : (t + 1) * gz, :].astype(f32)

    row = lax.broadcasted_iota(jnp.int32, (gz, LANES), 0)
    top, bottom = row == 0, row == gz - 1
    coup = [[coup_ref[d, e] for e in range(dofs)] for d in range(dofs)]

    def apply(src, at, dslot, emit):
        for y in range(gy):
            mid = [src[at, d * gy + y] for d in range(dofs)]
            dg = diag[dslot, y]
            for d in range(dofs):
                t = d * gy + y
                near = src[at - 1, t] + src[at + 1, t]
                if y > 0:
                    near = near + src[at, t - 1]
                if y < gy - 1:
                    near = near + src[at, t + 1]
                near = near + jnp.where(top, 0.0, pltpu.roll(mid[d], 1, 0))
                near = near + jnp.where(bottom, 0.0, pltpu.roll(mid[d], gz - 1, 0))
                total = (dg + coup[d][d]) * mid[d] - near
                for e in range(dofs):
                    if e != d:
                        total = total + coup[d][e] * mid[e]
                emit(t, total)

    def outside(layer):
        keep = jnp.where(layer < 0, low_in, jnp.where(layer >= layers, high_in, 1.0))
        return keep

    @pl.loop(0, layers + 4)
    def _(i):
        keep = outside(i - 2)

        def emit(t, total):
            s1[i, t] = total * keep

        apply(s0, i + 1, i, emit)

    @pl.loop(0, layers + 2)
    def _(i):
        keep = outside(i - 1)

        def emit(t, total):
            s2[i, t] = (total - 24.5 * s0[i + 2, t]) * keep

        apply(s1, i + 1, i + 1, emit)

    @pl.loop(0, layers)
    def _(i):
        def emit(t, total):
            last = (total - 12.25 * s1[i + 2, t]) * (4.0 / 343.0)
            out_ref[i % 2, i // 2, t * gz : (t + 1) * gz, :] = last.astype(bf16)

        apply(s2, i + 1, i + 2, emit)


def side_by_side(parts):
    return jnp.concatenate(parts, axis=1)


def gram_kernel(place_ref, dual_ref, far_dual_ref, f_ref, out_ref, send_ref):
    cores = f_ref.shape[0]
    pieces, height, _ = out_ref.shape
    each = pieces // cores
    here = place_ref[2]
    there = 1 - here
    part = 0.0
    for at, dual in ((here, dual_ref), (there, far_dual_ref)):
        pair = side_by_side([f_ref[b, at] for b in range(cores)])
        part = part + lax.dot_general(
            dual[...], pair, (((0,), (0,)), ((), ())), preferred_element_type=f32
        )
    for b in range(cores):
        cut = part[:, b * LANES : (b + 1) * LANES].astype(bf16)
        out_ref[b * each : (b + 1) * each] = cut.reshape(each, height, LANES)
        send_ref[b] = f_ref[b, there]


def sum_kernel(in_ref, out_ref):
    count = in_ref.shape[0]
    total = in_ref[0].astype(f32)
    for k in range(1, count):
        total = total + in_ref[k].astype(f32)
    piece = total.astype(bf16)
    for k in range(out_ref.shape[0]):
        out_ref[k] = piece


def rotate_kernel(scale, place_ref, f_ref, far_ref, g_ref, gram_ref, out_ref):
    cores = f_ref.shape[0]
    blocks = out_ref.shape[1] // LANES
    pieces, height, _ = g_ref.shape
    each = pieces // blocks
    half = each // 2
    own = each // blocks
    here = place_ref[2]
    mine = side_by_side([f_ref[b, here] for b in range(cores)])
    theirs = side_by_side([far_ref[b] for b in range(cores)])
    first = place_ref[3] * own

    def rows_of(k, at, many):
        return g_ref[pl.ds(k * each + at, many)].reshape(many * height, LANES)

    for b in range(0, blocks, 2):
        near = side_by_side([rows_of(k, here * half, half) for k in (b, b + 1)])
        far = side_by_side([rows_of(k, (1 - here) * half, half) for k in (b, b + 1)])
        turned = jnp.dot(mine, near, preferred_element_type=f32)
        turned = turned + jnp.dot(theirs, far, preferred_element_type=f32)
        out_ref[:, b * LANES : (b + 2) * LANES] = (turned * scale).astype(bf16)
        for k in (b, b + 1):
            gram_ref[:, k * LANES : (k + 1) * LANES] = rows_of(k, first, own).astype(f32)


def shards(vectors, node_shift, coupling, dual_basis):
    layers, dofs, gy, gz, width = vectors.shape
    rows = dofs * gy * gz
    count = lax.axis_size(NODES)
    near = lax.axis_size(NEAR)
    halves = lax.axis_size(HALVES)
    far = lax.axis_size(FAR)
    blocks = lax.axis_size(COLS)
    cols = blocks * width
    height = cols * blocks // (near * halves)
    v = vectors.reshape(layers, rows, width)
    shift_tile = jnp.pad(
        node_shift.transpose(2, 0, 1).reshape(gz, layers * gy), ((0, 0), (0, LANES - layers * gy))
    )
    message = jax.ShapeDtypeStruct((REACH * rows + gz, width), bf16)
    up, down = pl.pallas_call(
        pack_kernel, out_shape=(message, message), in_specs=vmem(2), out_specs=tuple(vmem(2)),
        compiler_params=room(8), name="pack",
    )(v, shift_tile)
    low = lax.ppermute(up, NODES, [(i, i + 1) for i in range(count - 1)])
    high = lax.ppermute(down, NODES, [(i + 1, i) for i in range(count - 1)])
    node = lax.axis_index(NODES)
    place = jnp.stack(
        [node > 0, node < count - 1, lax.axis_index(HALVES), lax.axis_index(COLS)]
    ).astype(jnp.int32)
    other = [(i, halves - 1 - i) for i in range(halves)]
    far_dual = lax.ppermute(dual_basis, HALVES, other)
    tiles = dofs * gy
    own = pl.pallas_call(
        functools.partial(filter_kernel, gy, dofs),
        out_shape=jax.ShapeDtypeStruct((layers // halves, halves, rows, width), bf16),
        in_specs=smem(2) + vmem(4),
        out_specs=vmem(1)[0],
        scratch_shapes=[
            pltpu.VMEM((layers + 6, tiles, gz, width), f32),
            pltpu.VMEM((layers + 4, tiles, gz, width), f32),
            pltpu.VMEM((layers + 2, tiles, gz, width), f32),
            pltpu.VMEM((layers + 4, gy, gz, width), f32),
        ],
        compiler_params=room(16), name="filter",
    )(coupling, place, v, low, high, shift_tile)
    mine = lax.all_to_all(own, "core", split_axis=0, concat_axis=0, tiled=True)
    terms, send = pl.pallas_call(
        gram_kernel,
        out_shape=(
            jax.ShapeDtypeStruct((near, height, LANES), bf16),
            jax.ShapeDtypeStruct((layers // halves, rows, width), bf16),
        ),
        in_specs=smem(1) + vmem(3), out_specs=tuple(vmem(2)), compiler_params=room(8), name="gram",
    )(place, dual_basis, far_dual, mine)
    theirs = lax.ppermute(send, HALVES, other)

    def summed(pieces, copies):
        return pl.pallas_call(
            sum_kernel,
            out_shape=jax.ShapeDtypeStruct((copies, height, LANES), bf16),
            in_specs=vmem(1), out_specs=vmem(1)[0], compiler_params=room(8),
        )(pieces)

    pieces = lax.all_to_all(terms, NEAR, split_axis=0, concat_axis=0, tiled=True)
    part = summed(pieces, far)
    pieces = lax.all_to_all(part, FAR, split_axis=0, concat_axis=0, tiled=True)
    everyone = (HALVES,) + NEAR
    full = summed(pieces, near * halves)
    pieces = lax.all_to_all(full, everyone, split_axis=0, concat_axis=0, tiled=True)
    gram, rotated = pl.pallas_call(
        functools.partial(rotate_kernel, cols ** (-0.5)),
        out_shape=(
            jax.ShapeDtypeStruct((cols // blocks, cols), f32),
            jax.ShapeDtypeStruct((rows, cols), bf16),
        ),
        in_specs=smem(1) + vmem(3), out_specs=tuple(vmem(2)), compiler_params=room(12), name="rotate",
    )(place, mine, theirs, pieces)
    return gram, rotated


SIZES = (2, 4, 8, 2, 2, 2)


def solution(mesh):
    torus = Mesh(mesh.devices.reshape(SIZES), NODES + COLS)
    placed = (P(NODES, None, None, None, COLS), P(NODES, None, None), P(), P(NODES + COLS, None))
    return jax.shard_map(
        shards,
        mesh=torus,
        in_specs=placed,
        out_specs=(P(COLS, None), P(NODES + COLS, None)),
        check_vma=False,
    )
```

```python
import functools

import jax
import jax.numpy as jnp
from jax import lax
from jax.experimental import pallas as pl
from jax.experimental.pallas import tpu as pltpu
from jax.sharding import Mesh
from jax.sharding import PartitionSpec as P


NODES = ("x_lo", "y", "z_hi", "z_lo")
COLS = ("x_hi", "core")
NEAR = ("x_lo", "y", "z_lo")
HALVES = "x_hi"
FAR = "z_hi"
REACH = 3
TILE_ROWS = 16
LANES = 128

bf16 = jnp.bfloat16
f32 = jnp.float32


def vmem(count):
    return [pl.BlockSpec(memory_space=pltpu.VMEM)] * count


def smem(count):
    return [pl.BlockSpec(memory_space=pltpu.SMEM)] * count


def room(mebibytes):
    return pltpu.CompilerParams(vmem_limit_bytes=mebibytes << 20)


def pack_kernel(v_ref, shift_ref, up_ref, down_ref):
    layers, rows = v_ref.shape[0], v_ref.shape[1]
    for k in range(REACH):
        up_ref[k * rows : (k + 1) * rows, :] = v_ref[layers - REACH + k]
        down_ref[k * rows : (k + 1) * rows, :] = v_ref[k]
    up_ref[REACH * rows :, :] = shift_ref[...]
    down_ref[REACH * rows :, :] = shift_ref[...]


def filter_kernel(
    gy, dofs, coup_ref, place_ref, v_ref, low_ref, high_ref, shift_ref, out_ref, s0, s1, s2, diag
):
    layers = v_ref.shape[0]
    gz = TILE_ROWS
    rows = dofs * gy * gz
    tiles = dofs * gy
    low_in = place_ref[0].astype(f32)
    high_in = place_ref[1].astype(f32)

    def shift_cols(ref, first, layer, slot):
        tile = ref[first : first + gz, :].astype(f32)
        for y in range(gy):
            k = layer * gy + y
            diag[slot, y] = jnp.broadcast_to(tile[:, k : k + 1], (gz, LANES)) - 4.0

    for k in range(2):
        shift_cols(low_ref, REACH * rows, layers - 2 + k, k)
        shift_cols(high_ref, REACH * rows, k, 2 + layers + k)
    for k in range(layers):
        shift_cols(shift_ref, 0, k, 2 + k)

    for t in range(tiles):
        for k in range(REACH):
            at = k * rows + t * gz
            s0[k, t] = low_ref[at : at + gz, :].astype(f32)
            s0[REACH + layers + k, t] = high_ref[at : at + gz, :].astype(f32)
        for k in range(layers):
            s0[REACH + k, t] = v_ref[k, t * gz : (t + 1) * gz, :].astype(f32)

    row = lax.broadcasted_iota(jnp.int32, (gz, LANES), 0)
    top, bottom = row == 0, row == gz - 1
    coup = [[coup_ref[d, e] for e in range(dofs)] for d in range(dofs)]

    def apply(src, at, dslot, emit):
        for y in range(gy):
            mid = [src[at, d * gy + y] for d in range(dofs)]
            dg = diag[dslot, y]
            for d in range(dofs):
                t = d * gy + y
                near = src[at - 1, t] + src[at + 1, t]
                if y > 0:
                    near = near + src[at, t - 1]
                if y < gy - 1:
                    near = near + src[at, t + 1]
                near = near + jnp.where(top, 0.0, pltpu.roll(mid[d], 1, 0))
                near = near + jnp.where(bottom, 0.0, pltpu.roll(mid[d], gz - 1, 0))
                total = (dg + coup[d][d]) * mid[d] - near
                for e in range(dofs):
                    if e != d:
                        total = total + coup[d][e] * mid[e]
                emit(t, total)

    def outside(layer):
        keep = jnp.where(layer < 0, low_in, jnp.where(layer >= layers, high_in, 1.0))
        return keep

    @pl.loop(0, layers + 4)
    def _(i):
        keep = outside(i - 2)

        def emit(t, total):
            s1[i, t] = total * keep

        apply(s0, i + 1, i, emit)

    @pl.loop(0, layers + 2)
    def _(i):
        keep = outside(i - 1)

        def emit(t, total):
            s2[i, t] = (total - 24.5 * s0[i + 2, t]) * keep

        apply(s1, i + 1, i + 1, emit)

    @pl.loop(0, layers)
    def _(i):
        def emit(t, total):
            last = (total - 12.25 * s1[i + 2, t]) * (4.0 / 343.0)
            out_ref[i, t * gz : (t + 1) * gz, :] = last.astype(bf16)

        apply(s2, i + 1, i + 2, emit)


def side_by_side(parts):
    return jnp.concatenate(parts, axis=1)


def gram_kernel(
    place_ref, own_ref, core_ref, half_ref, both_ref, f_ref, out_ref, to_core, to_half, to_both
):
    pieces, height, _ = out_ref.shape
    here, core = place_ref[2], place_ref[3]
    layers = [2 * a + b for a, b in spots(here, core)]
    part = 0.0
    for at, dual in zip(layers, (own_ref, core_ref, half_ref, both_ref)):
        part = part + lax.dot_general(
            f_ref[at], dual[...], (((0,), (0,)), ((), ())), preferred_element_type=f32
        )
    out_ref[...] = part.T.astype(bf16).reshape(pieces, height, LANES)
    for at, send in zip(layers[1:], (to_core, to_half, to_both)):
        send[...] = f_ref[at]


def spots(here, core):
    return (here, core), (here, 1 - core), (1 - here, core), (1 - here, 1 - core)


def sum_kernel(in_ref, out_ref):
    count = in_ref.shape[0]
    total = in_ref[0].astype(f32)
    for k in range(1, count):
        total = total + in_ref[k].astype(f32)
    piece = total.astype(bf16)
    for k in range(out_ref.shape[0]):
        out_ref[k] = piece


def rotate_kernel(scale, place_ref, f_ref, core_ref, half_ref, both_ref, g_ref, gram_ref, out_ref):
    blocks = out_ref.shape[1] // LANES
    pieces, height, _ = g_ref.shape
    each = pieces // blocks
    own = each // blocks
    here, core = place_ref[2], place_ref[3]
    places = [2 * a + b for a, b in spots(here, core)]
    cols = side_by_side([f_ref[places[0]], core_ref[...], half_ref[...], both_ref[...]])

    def rows_of(k, at):
        return g_ref[pl.ds(k * each + at * own, own)].reshape(own * height, LANES)

    for b in range(0, blocks, 2):
        turn = side_by_side(
            [jnp.concatenate([rows_of(k, at) for at in places], axis=0) for k in (b, b + 1)]
        )
        turned = jnp.dot(cols, turn, preferred_element_type=f32) * scale
        out_ref[:, b * LANES : (b + 2) * LANES] = turned.astype(bf16)
        for k in (b, b + 1):
            gram_ref[:, k * LANES : (k + 1) * LANES] = rows_of(k, places[0]).astype(f32)


def shards(vectors, node_shift, coupling, dual_basis):
    layers, dofs, gy, gz, width = vectors.shape
    rows = dofs * gy * gz
    count = lax.axis_size(NODES)
    near = lax.axis_size(NEAR)
    far = lax.axis_size(FAR)
    blocks = lax.axis_size(COLS)
    cols = blocks * width
    height = cols // near
    v = vectors.reshape(layers, rows, width)
    shift_tile = jnp.pad(
        node_shift.transpose(2, 0, 1).reshape(gz, layers * gy), ((0, 0), (0, LANES - layers * gy))
    )

    def swap(array, axes):
        many = lax.axis_size(axes)
        return lax.ppermute(array, axes, [(i, many - 1 - i) for i in range(many)])

    def spread(array, axes):
        return lax.all_to_all(array, axes, split_axis=0, concat_axis=0, tiled=True)

    dual_half = swap(dual_basis, HALVES)
    dual_core = swap(dual_basis, "core")
    message = jax.ShapeDtypeStruct((REACH * rows + gz, width), bf16)
    up, down = pl.pallas_call(
        pack_kernel, out_shape=(message, message), in_specs=vmem(2), out_specs=tuple(vmem(2)),
        compiler_params=room(8), name="pack",
    )(v, shift_tile)
    low = lax.ppermute(up, NODES, [(i, i + 1) for i in range(count - 1)])
    high = lax.ppermute(down, NODES, [(i + 1, i) for i in range(count - 1)])
    dual_both = swap(dual_half, "core")
    node = lax.axis_index(NODES)
    place = jnp.stack(
        [node > 0, node < count - 1, lax.axis_index(HALVES), lax.axis_index("core")]
    ).astype(jnp.int32)
    tiles = dofs * gy
    own = pl.pallas_call(
        functools.partial(filter_kernel, gy, dofs),
        out_shape=jax.ShapeDtypeStruct((layers, rows, width), bf16),
        in_specs=smem(2) + vmem(4),
        out_specs=vmem(1)[0],
        scratch_shapes=[
            pltpu.VMEM((layers + 6, tiles, gz, width), f32),
            pltpu.VMEM((layers + 4, tiles, gz, width), f32),
            pltpu.VMEM((layers + 2, tiles, gz, width), f32),
            pltpu.VMEM((layers + 4, gy, gz, width), f32),
        ],
        compiler_params=room(16), name="filter",
    )(coupling, place, v, low, high, shift_tile)
    layer = jax.ShapeDtypeStruct((rows, width), bf16)
    terms, to_core, to_half, to_both = pl.pallas_call(
        gram_kernel,
        out_shape=(jax.ShapeDtypeStruct((near, height, LANES), bf16), layer, layer, layer),
        in_specs=smem(1) + vmem(5), out_specs=tuple(vmem(4)), compiler_params=room(12), name="gram",
    )(place, dual_basis, dual_core, dual_half, dual_both, own)
    from_core = swap(to_core, "core")
    from_half = swap(to_half, HALVES)
    from_both = swap(to_both, COLS)

    def summed(pieces, copies):
        return pl.pallas_call(
            sum_kernel,
            out_shape=jax.ShapeDtypeStruct((copies, height, LANES), bf16),
            in_specs=vmem(1), out_specs=vmem(1)[0], compiler_params=room(8),
        )(pieces)

    pieces = spread(terms, NEAR)
    part = summed(pieces, far)
    pieces = spread(part, FAR)
    pieces = spread(summed(pieces, near * blocks), COLS + NEAR)
    gram, rotated = pl.pallas_call(
        functools.partial(rotate_kernel, cols ** (-0.5)),
        out_shape=(
            jax.ShapeDtypeStruct((cols // blocks, cols), f32),
            jax.ShapeDtypeStruct((rows, cols), bf16),
        ),
        in_specs=smem(1) + vmem(5), out_specs=tuple(vmem(2)), compiler_params=room(12), name="rotate",
    )(place, own, from_core, from_half, from_both, pieces)
    return gram, rotated


SIZES = (2, 4, 8, 2, 2, 2)


def solution(mesh):
    torus = Mesh(mesh.devices.reshape(SIZES), NODES + COLS)
    placed = (P(NODES, None, None, None, COLS), P(NODES, None, None), P(), P(NODES + COLS, None))
    return jax.shard_map(
        shards,
        mesh=torus,
        in_specs=placed,
        out_specs=(P(COLS, None), P(NODES + COLS, None)),
        check_vma=False,
    )
```

```python
import functools

import jax
import jax.numpy as jnp
from jax import lax
from jax.experimental import pallas as pl
from jax.experimental.pallas import tpu as pltpu
from jax.sharding import Mesh
from jax.sharding import PartitionSpec as P


NODES = ("x_lo", "y", "z_hi", "z_lo")
COLS = ("x_hi", "core")
NEAR = ("x_lo", "y", "z_lo")
HALVES = "x_hi"
FAR = "z_hi"
REACH = 3
TILE_ROWS = 16
LANES = 128
SHIFT_ROWS = 32

bf16 = jnp.bfloat16
f32 = jnp.float32


def vmem(count):
    return [pl.BlockSpec(memory_space=pltpu.VMEM)] * count


def smem(count):
    return [pl.BlockSpec(memory_space=pltpu.SMEM)] * count


def room(mebibytes):
    return pltpu.CompilerParams(vmem_limit_bytes=mebibytes << 20)


def pack_kernel(rows, v_ref, shift_ref, up_ref, down_ref, tile_ref, spread, sems):
    span = REACH * rows
    total = v_ref.shape[0]
    copies = [
        pltpu.make_async_copy(v_ref.at[total - span : total], up_ref.at[0:span], sems.at[0]),
        pltpu.make_async_copy(v_ref.at[0:span], down_ref.at[0:span], sems.at[1]),
    ]
    for copy in copies:
        copy.start()
    gy, layers, gz = shift_ref.shape
    spread[...] = jnp.zeros_like(spread)
    for y in range(gy):
        spread[y * layers : (y + 1) * layers, 0:gz] = shift_ref[y].astype(f32)
    tile = spread[...].astype(bf16)
    tile_ref[...] = tile
    up_ref[span:, :] = tile
    down_ref[span:, :] = tile
    for copy in copies:
        copy.wait()


def filter_kernel(
    gy, dofs, coup_ref, place_ref, v_ref, low_ref, high_ref, shift_ref, out_ref, s0, s1, s2, diag
):
    layers = v_ref.shape[0]
    gz = TILE_ROWS
    half = gz // 2
    rows = dofs * gy * gz
    tiles = dofs * gy
    span = REACH * rows

    stiff = jnp.concatenate(
        [low_ref[span:, :], shift_ref[...], high_ref[span:, :]]
        + [jnp.zeros((LANES - 3 * SHIFT_ROWS, LANES), bf16)],
        axis=0,
    )
    stiff = stiff.astype(f32).T
    firsts = [layers - 2 + k for k in range(2)]
    firsts += [SHIFT_ROWS + k for k in range(layers)]
    firsts += [2 * SHIFT_ROWS + k for k in range(2)]
    for slot, first in enumerate(firsts):
        for y in range(gy):
            lane = first + y * layers
            column = stiff[0:gz, lane : lane + 1]
            diag[slot, y] = jnp.broadcast_to(column, (gz, LANES)) - 4.0

    for t in range(tiles):
        for k in range(REACH):
            at = k * rows + t * gz
            s0[k, t] = low_ref[at : at + gz, :].astype(f32)
            s0[REACH + layers + k, t] = high_ref[at : at + gz, :].astype(f32)
        for k in range(layers):
            s0[REACH + k, t] = v_ref[k, t * gz : (t + 1) * gz, :].astype(f32)

    row = lax.broadcasted_iota(jnp.int32, (half, LANES), 0)
    top, bottom = row == 0, row == half - 1
    coup = [[coup_ref[d, e] for e in range(dofs)] for d in range(dofs)]
    halves = (slice(0, half), slice(half, gz))

    def apply(src, at, dslot, emit):
        for y in range(gy):
            mid = [[src[at, d * gy + y, part] for part in halves] for d in range(dofs)]
            dg = [diag[dslot, y, part] for part in halves]
            for d in range(dofs):
                t = d * gy + y
                up = [pltpu.roll(mid[d][k], 1, 0) for k in range(2)]
                down = [pltpu.roll(mid[d][k], half - 1, 0) for k in range(2)]
                shifted = (
                    jnp.where(top, 0.0, up[0]) + jnp.where(bottom, down[1], down[0]),
                    jnp.where(top, up[0], up[1]) + jnp.where(bottom, 0.0, down[1]),
                )
                for k, part in enumerate(halves):
                    near = src[at - 1, t, part] + src[at + 1, t, part]
                    if y > 0:
                        near = near + src[at, t - 1, part]
                    if y < gy - 1:
                        near = near + src[at, t + 1, part]
                    near = near + shifted[k]
                    total = (dg[k] + coup[d][d]) * mid[d][k] - near
                    for e in range(dofs):
                        if e != d:
                            total = total + coup[d][e] * mid[e][k]
                    emit(t, k, part, total)

    def clear(state, beyond):
        @pl.when(place_ref[0] == 0)
        def _():
            state[0:beyond] = jnp.zeros((beyond, tiles, gz, LANES), f32)

        @pl.when(place_ref[1] == 0)
        def _():
            state[layers + beyond :] = jnp.zeros((beyond, tiles, gz, LANES), f32)

    @pl.loop(0, layers + 4)
    def _(i):
        def emit(t, k, part, total):
            s1[i, t, part] = total

        apply(s0, i + 1, i, emit)

    clear(s1, 2)

    @pl.loop(0, layers + 2)
    def _(i):
        def emit(t, k, part, total):
            s2[i, t, part] = total - 24.5 * s0[i + 2, t, part]

        apply(s1, i + 1, i + 1, emit)

    clear(s2, 1)

    @pl.loop(0, layers)
    def _(i):
        held = {}

        def emit(t, k, part, total):
            held[k] = (total - 12.25 * s1[i + 2, t, part]) * (4.0 / 343.0)
            if k == 1:
                both = jnp.concatenate([held[0], held[1]], axis=0)
                out_ref[i, t * gz : (t + 1) * gz, :] = both.astype(bf16)

        apply(s2, i + 1, i + 2, emit)


def side_by_side(parts):
    return jnp.concatenate(parts, axis=1)


def gram_kernel(
    place_ref, own_ref, core_ref, half_ref, both_ref, f_ref, out_ref, to_core, to_half, to_both
):
    pieces, height, _ = out_ref.shape
    here, core = place_ref[2], place_ref[3]
    layers = [2 * a + b for a, b in spots(here, core)]
    part = 0.0
    for at, dual in zip(layers, (own_ref, core_ref, half_ref, both_ref)):
        part = part + lax.dot_general(
            f_ref[at], dual[...], (((0,), (0,)), ((), ())), preferred_element_type=f32
        )
    out_ref[...] = part.T.astype(bf16).reshape(pieces, height, LANES)
    for at, send in zip(layers[1:], (to_core, to_half, to_both)):
        send[...] = f_ref[at]


def spots(here, core):
    return (here, core), (here, 1 - core), (1 - here, core), (1 - here, 1 - core)


def sum_kernel(in_ref, out_ref):
    count = in_ref.shape[0]
    total = in_ref[0].astype(f32)
    for k in range(1, count):
        total = total + in_ref[k].astype(f32)
    piece = total.astype(bf16)
    for k in range(out_ref.shape[0]):
        out_ref[k] = piece


def rotate_kernel(scale, place_ref, f_ref, core_ref, half_ref, both_ref, g_ref, gram_ref, out_ref):
    blocks = out_ref.shape[1] // LANES
    pieces, height, _ = g_ref.shape
    each = pieces // blocks
    own = each // blocks
    here, core = place_ref[2], place_ref[3]
    places = [2 * a + b for a, b in spots(here, core)]
    cols = side_by_side([f_ref[places[0]], core_ref[...], half_ref[...], both_ref[...]])

    def rows_of(k, at):
        return g_ref[pl.ds(k * each + at * own, own)].reshape(own * height, LANES)

    for b in range(0, blocks, 2):
        turn = side_by_side(
            [jnp.concatenate([rows_of(k, at) for at in places], axis=0) for k in (b, b + 1)]
        )
        turned = jnp.dot(cols, turn, preferred_element_type=f32) * scale
        out_ref[:, b * LANES : (b + 2) * LANES] = turned.astype(bf16)
        for k in (b, b + 1):
            gram_ref[:, k * LANES : (k + 1) * LANES] = rows_of(k, places[0]).astype(f32)


def shards(vectors, node_shift, coupling, dual_basis):
    layers, dofs, gy, gz, width = vectors.shape
    rows = dofs * gy * gz
    count = lax.axis_size(NODES)
    near = lax.axis_size(NEAR)
    far = lax.axis_size(FAR)
    blocks = lax.axis_size(COLS)
    cols = blocks * width
    height = cols // near
    v = vectors.reshape(layers, rows, width)

    def swap(array, axes):
        many = lax.axis_size(axes)
        return lax.ppermute(array, axes, [(i, many - 1 - i) for i in range(many)])

    def spread(array, axes):
        return lax.all_to_all(array, axes, split_axis=0, concat_axis=0, tiled=True)

    dual_half = swap(dual_basis, HALVES)
    dual_core = swap(dual_basis, "core")
    message = jax.ShapeDtypeStruct((REACH * rows + SHIFT_ROWS, width), bf16)
    up, down, shift_tile = pl.pallas_call(
        functools.partial(pack_kernel, rows),
        out_shape=(message, message, jax.ShapeDtypeStruct((SHIFT_ROWS, width), bf16)),
        in_specs=[pl.BlockSpec(memory_space=pltpu.HBM)] + vmem(1), out_specs=tuple(vmem(3)),
        scratch_shapes=[pltpu.VMEM((SHIFT_ROWS, width), f32), pltpu.SemaphoreType.DMA((2,))],
        compiler_params=room(8), name="pack",
    )(vectors.reshape(layers * rows, width), node_shift.transpose(1, 0, 2))
    low = lax.ppermute(up, NODES, [(i, i + 1) for i in range(count - 1)])
    high = lax.ppermute(down, NODES, [(i + 1, i) for i in range(count - 1)])
    dual_both = swap(dual_half, "core")
    node = lax.axis_index(NODES)
    place = jnp.stack(
        [node > 0, node < count - 1, lax.axis_index(HALVES), lax.axis_index("core")]
    ).astype(jnp.int32)
    tiles = dofs * gy
    own = pl.pallas_call(
        functools.partial(filter_kernel, gy, dofs),
        out_shape=jax.ShapeDtypeStruct((layers, rows, width), bf16),
        in_specs=smem(2) + vmem(4),
        out_specs=vmem(1)[0],
        scratch_shapes=[
            pltpu.VMEM((layers + 6, tiles, gz, width), f32),
            pltpu.VMEM((layers + 4, tiles, gz, width), f32),
            pltpu.VMEM((layers + 2, tiles, gz, width), f32),
            pltpu.VMEM((layers + 4, gy, gz, width), f32),
        ],
        compiler_params=room(16), name="filter",
    )(coupling, place, v, low, high, shift_tile)
    layer = jax.ShapeDtypeStruct((rows, width), bf16)
    terms, to_core, to_half, to_both = pl.pallas_call(
        gram_kernel,
        out_shape=(jax.ShapeDtypeStruct((near, height, LANES), bf16), layer, layer, layer),
        in_specs=smem(1) + vmem(5), out_specs=tuple(vmem(4)), compiler_params=room(12), name="gram",
    )(place, dual_basis, dual_core, dual_half, dual_both, own)
    from_core = swap(to_core, "core")
    from_half = swap(to_half, HALVES)
    from_both = swap(to_both, COLS)

    def summed(pieces, copies):
        return pl.pallas_call(
            sum_kernel,
            out_shape=jax.ShapeDtypeStruct((copies, height, LANES), bf16),
            in_specs=vmem(1), out_specs=vmem(1)[0], compiler_params=room(8),
        )(pieces)

    pieces = spread(terms, NEAR)
    part = summed(pieces, far)
    pieces = spread(part, FAR)
    pieces = spread(summed(pieces, near * blocks), COLS + NEAR)
    gram, rotated = pl.pallas_call(
        functools.partial(rotate_kernel, cols ** (-0.5)),
        out_shape=(
            jax.ShapeDtypeStruct((cols // blocks, cols), f32),
            jax.ShapeDtypeStruct((rows, cols), bf16),
        ),
        in_specs=smem(1) + vmem(5), out_specs=tuple(vmem(2)), compiler_params=room(12), name="rotate",
    )(place, own, from_core, from_half, from_both, pieces)
    return gram, rotated


SIZES = (2, 4, 8, 2, 2, 2)


def solution(mesh):
    torus = Mesh(mesh.devices.reshape(SIZES), NODES + COLS)
    placed = (P(NODES, None, None, None, COLS), P(NODES, None, None), P(), P(NODES + COLS, None))
    return jax.shard_map(
        shards,
        mesh=torus,
        in_specs=placed,
        out_specs=(P(COLS, None), P(NODES + COLS, None)),
        check_vma=False,
    )
```

```python
import functools

import jax
import jax.numpy as jnp
from jax import lax
from jax.experimental import pallas as pl
from jax.experimental.pallas import tpu as pltpu
from jax.sharding import Mesh
from jax.sharding import PartitionSpec as P


NODES = ("x_lo", "y", "z_hi", "z_lo")
COLS = ("x_hi", "core")
NEAR = ("x_lo", "y", "z_lo")
HALVES = "x_hi"
FAR = "z_hi"
REACH = 3
TILE_ROWS = 16
LANES = 128
SHIFT_ROWS = 32

bf16 = jnp.bfloat16
f32 = jnp.float32


def vmem(count):
    return [pl.BlockSpec(memory_space=pltpu.VMEM)] * count


def smem(count):
    return [pl.BlockSpec(memory_space=pltpu.SMEM)] * count


def room(mebibytes):
    return pltpu.CompilerParams(vmem_limit_bytes=mebibytes << 20)


def pack_kernel(rows, v_ref, shift_ref, up_ref, down_ref, tile_ref, spread, sems):
    span = REACH * rows
    total = v_ref.shape[0]
    copies = [
        pltpu.make_async_copy(v_ref.at[total - span : total], up_ref.at[0:span], sems.at[0]),
        pltpu.make_async_copy(v_ref.at[0:span], down_ref.at[0:span], sems.at[1]),
    ]
    for copy in copies:
        copy.start()
    gy, layers, gz = shift_ref.shape
    spread[...] = jnp.zeros_like(spread)
    for y in range(gy):
        spread[y * layers : (y + 1) * layers, 0:gz] = shift_ref[y].astype(f32)
    tile = spread[...].astype(bf16)
    tile_ref[...] = tile
    up_ref[span:, :] = tile
    down_ref[span:, :] = tile
    for copy in copies:
        copy.wait()


def filter_kernel(
    gy, dofs, coup_ref, place_ref, v_ref, low_ref, high_ref, shift_ref, out_ref, s0, s1, s2, diag
):
    layers = v_ref.shape[0]
    gz = TILE_ROWS
    half = gz // 2
    rows = dofs * gy * gz
    tiles = dofs * gy
    span = REACH * rows

    stiff = jnp.concatenate(
        [low_ref[span:, :], shift_ref[...], high_ref[span:, :]]
        + [jnp.zeros((LANES - 3 * SHIFT_ROWS, LANES), bf16)],
        axis=0,
    )
    stiff = stiff.astype(f32).T
    firsts = [layers - 2 + k for k in range(2)]
    firsts += [SHIFT_ROWS + k for k in range(layers)]
    firsts += [2 * SHIFT_ROWS + k for k in range(2)]
    for slot, first in enumerate(firsts):
        for y in range(gy):
            lane = first + y * layers
            column = stiff[0:gz, lane : lane + 1]
            diag[slot, y] = jnp.broadcast_to(column, (gz, LANES)) - 4.0

    for t in range(tiles):
        for k in range(REACH):
            at = k * rows + t * gz
            s0[k, t] = low_ref[at : at + gz, :].astype(f32)
            s0[REACH + layers + k, t] = high_ref[at : at + gz, :].astype(f32)
        for k in range(layers):
            s0[REACH + k, t] = v_ref[k, t * gz : (t + 1) * gz, :].astype(f32)

    row = lax.broadcasted_iota(jnp.int32, (half, LANES), 0)
    top, bottom = row == 0, row == half - 1
    coup = [[coup_ref[d, e] for e in range(dofs)] for d in range(dofs)]
    halves = (slice(0, half), slice(half, gz))

    def apply(src, at, dslot, emit):
        for y in range(gy):
            mid = [[src[at, d * gy + y, part] for part in halves] for d in range(dofs)]
            dg = [diag[dslot, y, part] for part in halves]
            for d in range(dofs):
                t = d * gy + y
                up = [pltpu.roll(mid[d][k], 1, 0) for k in range(2)]
                down = [pltpu.roll(mid[d][k], half - 1, 0) for k in range(2)]
                shifted = (
                    jnp.where(top, 0.0, up[0]) + jnp.where(bottom, down[1], down[0]),
                    jnp.where(top, up[0], up[1]) + jnp.where(bottom, 0.0, down[1]),
                )
                for k, part in enumerate(halves):
                    near = src[at - 1, t, part] + src[at + 1, t, part]
                    if y > 0:
                        near = near + src[at, t - 1, part]
                    if y < gy - 1:
                        near = near + src[at, t + 1, part]
                    near = near + shifted[k]
                    total = (dg[k] + coup[d][d]) * mid[d][k] - near
                    for e in range(dofs):
                        if e != d:
                            total = total + coup[d][e] * mid[e][k]
                    emit(t, k, part, total)

    def clear(state, beyond):
        @pl.when(place_ref[0] == 0)
        def _():
            state[0:beyond] = jnp.zeros((beyond, tiles, gz, LANES), f32)

        @pl.when(place_ref[1] == 0)
        def _():
            state[layers + beyond :] = jnp.zeros((beyond, tiles, gz, LANES), f32)

    @pl.loop(0, layers + 4)
    def _(i):
        def emit(t, k, part, total):
            s1[i, t, part] = total

        apply(s0, i + 1, i, emit)

    clear(s1, 2)

    @pl.loop(0, layers + 2)
    def _(i):
        def emit(t, k, part, total):
            s2[i, t, part] = total - 24.5 * s0[i + 2, t, part]

        apply(s1, i + 1, i + 1, emit)

    clear(s2, 1)

    @pl.loop(0, layers)
    def _(i):
        held = {}

        def emit(t, k, part, total):
            held[k] = (total - 12.25 * s1[i + 2, t, part]) * (4.0 / 343.0)
            if k == 1:
                both = jnp.concatenate([held[0], held[1]], axis=0)
                out_ref[i, t * gz : (t + 1) * gz, :] = both.astype(bf16)

        apply(s2, i + 1, i + 2, emit)


def side_by_side(parts):
    return jnp.concatenate(parts, axis=1)


def gram_kernel(
    place_ref, own_ref, core_ref, half_ref, both_ref, f_ref, out_ref, to_half
):
    pieces, height, _ = out_ref.shape
    here, core = place_ref[2], place_ref[3]
    layers = [2 * a + b for a, b in spots(here, core)]
    part = 0.0
    for at, dual in zip(layers, (own_ref, core_ref, half_ref, both_ref)):
        part = part + lax.dot_general(
            f_ref[at], dual[...], (((0,), (0,)), ((), ())), preferred_element_type=f32
        )
    out_ref[...] = part.T.astype(bf16).reshape(pieces, height, LANES)
    first = 2 * (1 - here)
    to_half[...] = f_ref[pl.ds(first, 2)]


def spots(here, core):
    return (here, core), (here, 1 - core), (1 - here, core), (1 - here, 1 - core)


def sum_kernel(in_ref, out_ref):
    count = in_ref.shape[0]
    total = in_ref[0].astype(f32)
    for k in range(1, count):
        total = total + in_ref[k].astype(f32)
    piece = total.astype(bf16)
    for k in range(out_ref.shape[0]):
        out_ref[k] = piece


def far_sum_kernel(place_ref, in_ref, f_ref, half_ref, out_ref, to_core):
    sum_kernel(in_ref, out_ref)
    here, core = place_ref[2], place_ref[3]
    to_core[0] = f_ref[2 * here + 1 - core]
    to_core[1] = half_ref[1 - core]


def rows_of(g_ref, half, at):
    pieces, height, _ = g_ref.shape
    each = pieces // 2
    own = LANES // height
    return g_ref[pl.ds(half * each + at * own, own)].reshape(LANES, LANES)


def rotated_half(scale, place_ref, f_ref, half_ref, core_ref, g_ref):
    here, core = place_ref[2], place_ref[3]
    places = [
        2 * here + core,
        2 * (1 - here) + core,
        2 * here + 1 - core,
        2 * (1 - here) + 1 - core,
    ]
    cols = side_by_side([f_ref[places[0]], half_ref[core], core_ref[0], core_ref[1]])
    turn = side_by_side(
        [jnp.concatenate([rows_of(g_ref, k, at) for at in places], axis=0) for k in range(2)]
    )
    return (jnp.dot(cols, turn, preferred_element_type=f32) * scale).astype(bf16)


def rotate_half_kernel(scale, place_ref, f_ref, half_ref, core_ref, g_ref, out_ref):
    out_ref[...] = rotated_half(scale, place_ref, f_ref, half_ref, core_ref, g_ref)


def rotate_kernel(
    scale, place_ref, f_ref, half_ref, core_ref, g_ref, far_ref, done_ref, gram_ref, out_ref
):
    here, core = place_ref[2], place_ref[3]
    other = rotated_half(scale, place_ref, f_ref, half_ref, core_ref, far_ref)
    for k in range(2):
        cut = slice(k * LANES, (k + 1) * LANES)
        mine = pl.ds(pl.multiple_of((2 * k + core) * LANES, LANES), LANES)
        theirs = pl.ds(pl.multiple_of((2 * k + 1 - core) * LANES, LANES), LANES)
        out_ref[:, mine] = done_ref[:, cut]
        out_ref[:, theirs] = other[:, cut]
        at = 2 * here + core
        gram_ref[:, mine] = rows_of(g_ref, k, at).astype(f32)
        gram_ref[:, theirs] = rows_of(far_ref, k, at).astype(f32)


def shards(vectors, node_shift, coupling, dual_basis):
    layers, dofs, gy, gz, width = vectors.shape
    rows = dofs * gy * gz
    count = lax.axis_size(NODES)
    near = lax.axis_size(NEAR)
    far = lax.axis_size(FAR)
    blocks = lax.axis_size(COLS)
    cols = blocks * width
    height = cols // near
    v = vectors.reshape(layers, rows, width)

    def swap(array, axes):
        many = lax.axis_size(axes)
        return lax.ppermute(array, axes, [(i, many - 1 - i) for i in range(many)])

    def spread(array, axes):
        return lax.all_to_all(array, axes, split_axis=0, concat_axis=0, tiled=True)

    dual_half = swap(dual_basis, HALVES)
    dual_core = swap(dual_basis, "core")
    message = jax.ShapeDtypeStruct((REACH * rows + SHIFT_ROWS, width), bf16)
    up, down, shift_tile = pl.pallas_call(
        functools.partial(pack_kernel, rows),
        out_shape=(message, message, jax.ShapeDtypeStruct((SHIFT_ROWS, width), bf16)),
        in_specs=[pl.BlockSpec(memory_space=pltpu.HBM)] + vmem(1), out_specs=tuple(vmem(3)),
        scratch_shapes=[pltpu.VMEM((SHIFT_ROWS, width), f32), pltpu.SemaphoreType.DMA((2,))],
        compiler_params=room(8), name="pack",
    )(vectors.reshape(layers * rows, width), node_shift.transpose(1, 0, 2))
    low = lax.ppermute(up, NODES, [(i, i + 1) for i in range(count - 1)])
    high = lax.ppermute(down, NODES, [(i + 1, i) for i in range(count - 1)])
    dual_both = swap(dual_half, "core")
    node = lax.axis_index(NODES)
    place = jnp.stack(
        [node > 0, node < count - 1, lax.axis_index(HALVES), lax.axis_index("core")]
    ).astype(jnp.int32)
    tiles = dofs * gy
    own = pl.pallas_call(
        functools.partial(filter_kernel, gy, dofs),
        out_shape=jax.ShapeDtypeStruct((layers, rows, width), bf16),
        in_specs=smem(2) + vmem(4),
        out_specs=vmem(1)[0],
        scratch_shapes=[
            pltpu.VMEM((layers + 6, tiles, gz, width), f32),
            pltpu.VMEM((layers + 4, tiles, gz, width), f32),
            pltpu.VMEM((layers + 2, tiles, gz, width), f32),
            pltpu.VMEM((layers + 4, gy, gz, width), f32),
        ],
        compiler_params=room(16), name="filter",
    )(coupling, place, v, low, high, shift_tile)
    two = jax.ShapeDtypeStruct((2, rows, width), bf16)
    terms, to_half = pl.pallas_call(
        gram_kernel,
        out_shape=(jax.ShapeDtypeStruct((near, height, LANES), bf16), two),
        in_specs=smem(1) + vmem(5), out_specs=tuple(vmem(2)), compiler_params=room(12), name="gram",
    )(place, dual_basis, dual_core, dual_half, dual_both, own)
    from_half = swap(to_half, HALVES)
    pieces = spread(terms, NEAR)
    part = pl.pallas_call(
        sum_kernel,
        out_shape=jax.ShapeDtypeStruct((far, height, LANES), bf16),
        in_specs=vmem(1), out_specs=vmem(1)[0], compiler_params=room(8), name="near_sum",
    )(pieces)
    pieces = spread(part, FAR)
    full, to_core = pl.pallas_call(
        far_sum_kernel,
        out_shape=(jax.ShapeDtypeStruct((2 * near, height, LANES), bf16), two),
        in_specs=smem(1) + vmem(3), out_specs=tuple(vmem(2)), compiler_params=room(8), name="far_sum",
    )(place, pieces, own, from_half)
    from_core = swap(to_core, "core")
    pieces = spread(full, (HALVES,) + NEAR)
    other = swap(pieces, "core")
    scale = cols ** (-0.5)
    half = pl.pallas_call(
        functools.partial(rotate_half_kernel, scale),
        out_shape=jax.ShapeDtypeStruct((rows, cols // 2), bf16),
        in_specs=smem(1) + vmem(4), out_specs=vmem(1)[0], compiler_params=room(8),
        name="rotate_half",
    )(place, own, from_half, from_core, pieces)
    gram, rotated = pl.pallas_call(
        functools.partial(rotate_kernel, scale),
        out_shape=(
            jax.ShapeDtypeStruct((cols // blocks, cols), f32),
            jax.ShapeDtypeStruct((rows, cols), bf16),
        ),
        in_specs=smem(1) + vmem(6), out_specs=tuple(vmem(2)), compiler_params=room(12), name="rotate",
    )(place, own, from_half, from_core, pieces, other, half)
    return gram, rotated


SIZES = (2, 4, 8, 2, 2, 2)


def solution(mesh):
    torus = Mesh(mesh.devices.reshape(SIZES), NODES + COLS)
    placed = (P(NODES, None, None, None, COLS), P(NODES, None, None), P(), P(NODES + COLS, None))
    return jax.shard_map(
        shards,
        mesh=torus,
        in_specs=placed,
        out_specs=(P(COLS, None), P(NODES + COLS, None)),
        check_vma=False,
    )
```

```python
import functools

import jax
import jax.numpy as jnp
from jax import lax
from jax.experimental import pallas as pl
from jax.experimental.pallas import tpu as pltpu
from jax.sharding import Mesh
from jax.sharding import PartitionSpec as P


NODES = ("x_lo", "y", "z_hi", "z_lo")
COLS = ("x_hi", "core")
NEAR = ("x_lo", "y", "z_lo")
HALVES = "x_hi"
FAR = "z_hi"
REACH = 3
TILE_ROWS = 16
LANES = 128
SHIFT_ROWS = 32

bf16 = jnp.bfloat16
f32 = jnp.float32


def vmem(count):
    return [pl.BlockSpec(memory_space=pltpu.VMEM)] * count


def smem(count):
    return [pl.BlockSpec(memory_space=pltpu.SMEM)] * count


def room(mebibytes):
    return pltpu.CompilerParams(vmem_limit_bytes=mebibytes << 20)


def pack_kernel(rows, v_ref, shift_ref, up_ref, down_ref, tile_ref, spread, sems):
    span = REACH * rows
    total = v_ref.shape[0]
    copies = [
        pltpu.make_async_copy(v_ref.at[total - span : total], up_ref.at[0:span], sems.at[0]),
        pltpu.make_async_copy(v_ref.at[0:span], down_ref.at[0:span], sems.at[1]),
    ]
    for copy in copies:
        copy.start()
    gy, layers, gz = shift_ref.shape
    spread[...] = jnp.zeros_like(spread)
    for y in range(gy):
        spread[y * layers : (y + 1) * layers, 0:gz] = shift_ref[y].astype(f32)
    tile = spread[...].astype(bf16)
    tile_ref[...] = tile
    up_ref[span:, :] = tile
    down_ref[span:, :] = tile
    for copy in copies:
        copy.wait()


def filter_kernel(
    gy, dofs, coup_ref, place_ref, v_ref, low_ref, high_ref, shift_ref, out_ref, s0, s1, s2, diag
):
    layers = v_ref.shape[0]
    gz = TILE_ROWS
    half = gz // 2
    rows = dofs * gy * gz
    tiles = dofs * gy
    span = REACH * rows

    stiff = jnp.concatenate(
        [low_ref[span:, :], shift_ref[...], high_ref[span:, :]]
        + [jnp.zeros((LANES - 3 * SHIFT_ROWS, LANES), bf16)],
        axis=0,
    )
    stiff = stiff.astype(f32).T
    firsts = [layers - 2 + k for k in range(2)]
    firsts += [SHIFT_ROWS + k for k in range(layers)]
    firsts += [2 * SHIFT_ROWS + k for k in range(2)]
    for slot, first in enumerate(firsts):
        for y in range(gy):
            lane = first + y * layers
            column = stiff[0:gz, lane : lane + 1]
            diag[slot, y] = jnp.broadcast_to(column, (gz, LANES)) - 4.0

    for t in range(tiles):
        for k in range(REACH):
            at = k * rows + t * gz
            s0[k, t] = low_ref[at : at + gz, :].astype(f32)
            s0[REACH + layers + k, t] = high_ref[at : at + gz, :].astype(f32)
        for k in range(layers):
            s0[REACH + k, t] = v_ref[k, t * gz : (t + 1) * gz, :].astype(f32)

    row = lax.broadcasted_iota(jnp.int32, (half, LANES), 0)
    top, bottom = row == 0, row == half - 1
    coup = [[coup_ref[d, e] for e in range(dofs)] for d in range(dofs)]
    halves = (slice(0, half), slice(half, gz))

    def apply(src, at, dslot, emit):
        for y in range(gy):
            mid = [[src[at, d * gy + y, part] for part in halves] for d in range(dofs)]
            dg = [diag[dslot, y, part] for part in halves]
            for d in range(dofs):
                t = d * gy + y
                up = [pltpu.roll(mid[d][k], 1, 0) for k in range(2)]
                down = [pltpu.roll(mid[d][k], half - 1, 0) for k in range(2)]
                shifted = (
                    jnp.where(top, 0.0, up[0]) + jnp.where(bottom, down[1], down[0]),
                    jnp.where(top, up[0], up[1]) + jnp.where(bottom, 0.0, down[1]),
                )
                for k, part in enumerate(halves):
                    near = src[at - 1, t, part] + src[at + 1, t, part]
                    if y > 0:
                        near = near + src[at, t - 1, part]
                    if y < gy - 1:
                        near = near + src[at, t + 1, part]
                    near = near + shifted[k]
                    total = (dg[k] + coup[d][d]) * mid[d][k] - near
                    for e in range(dofs):
                        if e != d:
                            total = total + coup[d][e] * mid[e][k]
                    emit(t, k, part, total)

    def clear(state, beyond):
        @pl.when(place_ref[0] == 0)
        def _():
            state[0:beyond] = jnp.zeros((beyond, tiles, gz, LANES), f32)

        @pl.when(place_ref[1] == 0)
        def _():
            state[layers + beyond :] = jnp.zeros((beyond, tiles, gz, LANES), f32)

    @pl.loop(0, layers + 4)
    def _(i):
        def emit(t, k, part, total):
            s1[i, t, part] = total

        apply(s0, i + 1, i, emit)

    clear(s1, 2)

    @pl.loop(0, layers + 2)
    def _(i):
        def emit(t, k, part, total):
            s2[i, t, part] = total - 24.5 * s0[i + 2, t, part]

        apply(s1, i + 1, i + 1, emit)

    clear(s2, 1)

    @pl.loop(0, layers)
    def _(i):
        held = {}

        def emit(t, k, part, total):
            held[k] = (total - 12.25 * s1[i + 2, t, part]) * (4.0 / 343.0)
            if k == 1:
                both = jnp.concatenate([held[0], held[1]], axis=0)
                out_ref[i, t * gz : (t + 1) * gz, :] = both.astype(bf16)

        apply(s2, i + 1, i + 2, emit)


def side_by_side(parts):
    return jnp.concatenate(parts, axis=1)


def gram_kernel(
    place_ref, own_ref, core_ref, half_ref, both_ref, f_ref, out_ref, to_half
):
    pieces, height, _ = out_ref.shape
    here, core = place_ref[2], place_ref[3]
    layers = [2 * a + b for a, b in spots(here, core)]
    part = 0.0
    for at, dual in zip(layers, (own_ref, core_ref, half_ref, both_ref)):
        part = part + lax.dot_general(
            f_ref[at], dual[...], (((0,), (0,)), ((), ())), preferred_element_type=f32
        )
    out_ref[...] = part.T.astype(bf16).reshape(pieces, height, LANES)
    first = 2 * (1 - here)
    to_half[...] = f_ref[pl.ds(first, 2)]


def spots(here, core):
    return (here, core), (here, 1 - core), (1 - here, core), (1 - here, 1 - core)


def sum_kernel(in_ref, out_ref):
    count = in_ref.shape[0]
    total = in_ref[0].astype(f32)
    for k in range(1, count):
        total = total + in_ref[k].astype(f32)
    piece = total.astype(bf16)
    for k in range(out_ref.shape[0]):
        out_ref[k] = piece


def pick_kernel(place_ref, f_ref, half_ref, to_core):
    here, core = place_ref[2], place_ref[3]
    to_core[0] = f_ref[2 * here + 1 - core]
    to_core[1] = half_ref[1 - core]


def rotate_kernel(scale, place_ref, f_ref, half_ref, core_ref, g_ref, gram_ref, out_ref):
    blocks = out_ref.shape[1] // LANES
    pieces, height, _ = g_ref.shape
    each = pieces // blocks
    own = each // blocks
    here, core = place_ref[2], place_ref[3]
    places = [
        2 * here + core,
        2 * (1 - here) + core,
        2 * here + 1 - core,
        2 * (1 - here) + 1 - core,
    ]
    cols = side_by_side([f_ref[places[0]], half_ref[core], core_ref[0], core_ref[1]])

    def rows_of(k, at):
        return g_ref[pl.ds(k * each + at * own, own)].reshape(own * height, LANES)

    for b in range(0, blocks, 2):
        turn = side_by_side(
            [jnp.concatenate([rows_of(k, at) for at in places], axis=0) for k in (b, b + 1)]
        )
        turned = jnp.dot(cols, turn, preferred_element_type=f32) * scale
        out_ref[:, b * LANES : (b + 2) * LANES] = turned.astype(bf16)
        for k in (b, b + 1):
            gram_ref[:, k * LANES : (k + 1) * LANES] = rows_of(k, places[0]).astype(f32)


def shards(vectors, node_shift, coupling, dual_basis):
    layers, dofs, gy, gz, width = vectors.shape
    rows = dofs * gy * gz
    count = lax.axis_size(NODES)
    near = lax.axis_size(NEAR)
    far = lax.axis_size(FAR)
    blocks = lax.axis_size(COLS)
    cols = blocks * width
    height = cols // near
    v = vectors.reshape(layers, rows, width)

    def swap(array, axes):
        many = lax.axis_size(axes)
        return lax.ppermute(array, axes, [(i, many - 1 - i) for i in range(many)])

    def spread(array, axes):
        return lax.all_to_all(array, axes, split_axis=0, concat_axis=0, tiled=True)

    dual_half = swap(dual_basis, HALVES)
    dual_core = swap(dual_basis, "core")
    message = jax.ShapeDtypeStruct((REACH * rows + SHIFT_ROWS, width), bf16)
    up, down, shift_tile = pl.pallas_call(
        functools.partial(pack_kernel, rows),
        out_shape=(message, message, jax.ShapeDtypeStruct((SHIFT_ROWS, width), bf16)),
        in_specs=[pl.BlockSpec(memory_space=pltpu.HBM)] + vmem(1), out_specs=tuple(vmem(3)),
        scratch_shapes=[pltpu.VMEM((SHIFT_ROWS, width), f32), pltpu.SemaphoreType.DMA((2,))],
        compiler_params=room(8), name="pack",
    )(vectors.reshape(layers * rows, width), node_shift.transpose(1, 0, 2))
    low = lax.ppermute(up, NODES, [(i, i + 1) for i in range(count - 1)])
    high = lax.ppermute(down, NODES, [(i + 1, i) for i in range(count - 1)])
    dual_both = swap(dual_half, "core")
    node = lax.axis_index(NODES)
    place = jnp.stack(
        [node > 0, node < count - 1, lax.axis_index(HALVES), lax.axis_index("core")]
    ).astype(jnp.int32)
    tiles = dofs * gy
    own = pl.pallas_call(
        functools.partial(filter_kernel, gy, dofs),
        out_shape=jax.ShapeDtypeStruct((layers, rows, width), bf16),
        in_specs=smem(2) + vmem(4),
        out_specs=vmem(1)[0],
        scratch_shapes=[
            pltpu.VMEM((layers + 6, tiles, gz, width), f32),
            pltpu.VMEM((layers + 4, tiles, gz, width), f32),
            pltpu.VMEM((layers + 2, tiles, gz, width), f32),
            pltpu.VMEM((layers + 4, gy, gz, width), f32),
        ],
        compiler_params=room(16), name="filter",
    )(coupling, place, v, low, high, shift_tile)
    two = jax.ShapeDtypeStruct((2, rows, width), bf16)
    terms, to_half = pl.pallas_call(
        gram_kernel,
        out_shape=(jax.ShapeDtypeStruct((near, height, LANES), bf16), two),
        in_specs=smem(1) + vmem(5), out_specs=tuple(vmem(2)), compiler_params=room(12), name="gram",
    )(place, dual_basis, dual_core, dual_half, dual_both, own)
    from_half = swap(to_half, HALVES)
    pieces = spread(terms, NEAR)
    to_core = pl.pallas_call(
        pick_kernel,
        out_shape=two,
        in_specs=smem(1) + vmem(2), out_specs=vmem(1)[0], compiler_params=room(8), name="pick",
    )(place, own, from_half)
    from_core = swap(to_core, "core")

    def summed(pieces, copies):
        return pl.pallas_call(
            sum_kernel,
            out_shape=jax.ShapeDtypeStruct((copies, height, LANES), bf16),
            in_specs=vmem(1), out_specs=vmem(1)[0], compiler_params=room(8),
        )(pieces)

    pieces = spread(summed(pieces, far), FAR)
    pieces = spread(summed(pieces, near * blocks), COLS + NEAR)
    gram, rotated = pl.pallas_call(
        functools.partial(rotate_kernel, cols ** (-0.5)),
        out_shape=(
            jax.ShapeDtypeStruct((cols // blocks, cols), f32),
            jax.ShapeDtypeStruct((rows, cols), bf16),
        ),
        in_specs=smem(1) + vmem(4), out_specs=tuple(vmem(2)), compiler_params=room(12), name="rotate",
    )(place, own, from_half, from_core, pieces)
    return gram, rotated


SIZES = (2, 4, 8, 2, 2, 2)


def solution(mesh):
    torus = Mesh(mesh.devices.reshape(SIZES), NODES + COLS)
    placed = (P(NODES, None, None, None, COLS), P(NODES, None, None), P(), P(NODES + COLS, None))
    return jax.shard_map(
        shards,
        mesh=torus,
        in_specs=placed,
        out_specs=(P(COLS, None), P(NODES + COLS, None)),
        check_vma=False,
    )
```

```python
import functools

import jax
import jax.numpy as jnp
from jax import lax
from jax.experimental import pallas as pl
from jax.experimental.pallas import tpu as pltpu
from jax.sharding import Mesh
from jax.sharding import PartitionSpec as P


NODES = ("x_lo", "y", "z_hi", "z_lo")
COLS = ("x_hi", "core")
NEAR = ("x_lo", "y", "z_lo")
HALVES = "x_hi"
FAR = "z_hi"
REACH = 3
TILE_ROWS = 16
LANES = 128
SHIFT_ROWS = 32

bf16 = jnp.bfloat16
f32 = jnp.float32


def vmem(count):
    return [pl.BlockSpec(memory_space=pltpu.VMEM)] * count


def smem(count):
    return [pl.BlockSpec(memory_space=pltpu.SMEM)] * count


def room(mebibytes):
    return pltpu.CompilerParams(vmem_limit_bytes=mebibytes << 20)


def pack_kernel(rows, v_ref, shift_ref, up_ref, down_ref, tile_ref, spread, sems):
    span = REACH * rows
    total = v_ref.shape[0]
    copies = [
        pltpu.make_async_copy(v_ref.at[total - span : total], up_ref.at[0:span], sems.at[0]),
        pltpu.make_async_copy(v_ref.at[0:span], down_ref.at[0:span], sems.at[1]),
    ]
    for copy in copies:
        copy.start()
    gy, layers, gz = shift_ref.shape
    spread[...] = jnp.zeros_like(spread)
    for y in range(gy):
        spread[y * layers : (y + 1) * layers, 0:gz] = shift_ref[y].astype(f32)
    tile = spread[...].astype(bf16)
    tile_ref[...] = tile
    up_ref[span:, :] = tile
    down_ref[span:, :] = tile
    for copy in copies:
        copy.wait()


def filter_kernel(
    gy, dofs, coup_ref, place_ref, v_ref, low_ref, high_ref, shift_ref, out_ref, s0, s1, s2, diag
):
    layers = v_ref.shape[0]
    gz = TILE_ROWS
    half = gz // 2
    rows = dofs * gy * gz
    tiles = dofs * gy
    span = REACH * rows

    stiff = jnp.concatenate(
        [low_ref[span:, :], shift_ref[...], high_ref[span:, :]]
        + [jnp.zeros((LANES - 3 * SHIFT_ROWS, LANES), bf16)],
        axis=0,
    )
    stiff = stiff.astype(f32).T
    firsts = [layers - 2 + k for k in range(2)]
    firsts += [SHIFT_ROWS + k for k in range(layers)]
    firsts += [2 * SHIFT_ROWS + k for k in range(2)]
    for slot, first in enumerate(firsts):
        for y in range(gy):
            lane = first + y * layers
            column = stiff[0:gz, lane : lane + 1]
            diag[slot, y] = jnp.broadcast_to(column, (gz, LANES)) - 4.0

    for t in range(tiles):
        for k in range(REACH):
            at = k * rows + t * gz
            s0[k, t] = low_ref[at : at + gz, :].astype(f32)
            s0[REACH + layers + k, t] = high_ref[at : at + gz, :].astype(f32)
        for k in range(layers):
            s0[REACH + k, t] = v_ref[k, t * gz : (t + 1) * gz, :].astype(f32)

    row = lax.broadcasted_iota(jnp.int32, (half, LANES), 0)
    top, bottom = row == 0, row == half - 1
    coup = [[coup_ref[d, e] for e in range(dofs)] for d in range(dofs)]
    halves = (slice(0, half), slice(half, gz))

    def apply(src, at, dslot, emit):
        for y in range(gy):
            mid = [[src[at, d * gy + y, part] for part in halves] for d in range(dofs)]
            dg = [diag[dslot, y, part] for part in halves]
            for d in range(dofs):
                t = d * gy + y
                up = [pltpu.roll(mid[d][k], 1, 0) for k in range(2)]
                down = [pltpu.roll(mid[d][k], half - 1, 0) for k in range(2)]
                shifted = (
                    jnp.where(top, 0.0, up[0]) + jnp.where(bottom, down[1], down[0]),
                    jnp.where(top, up[0], up[1]) + jnp.where(bottom, 0.0, down[1]),
                )
                for k, part in enumerate(halves):
                    near = src[at - 1, t, part] + src[at + 1, t, part]
                    if y > 0:
                        near = near + src[at, t - 1, part]
                    if y < gy - 1:
                        near = near + src[at, t + 1, part]
                    near = near + shifted[k]
                    total = (dg[k] + coup[d][d]) * mid[d][k] - near
                    for e in range(dofs):
                        if e != d:
                            total = total + coup[d][e] * mid[e][k]
                    emit(t, k, part, total)

    def clear(state, beyond):
        @pl.when(place_ref[0] == 0)
        def _():
            state[0:beyond] = jnp.zeros((beyond, tiles, gz, LANES), f32)

        @pl.when(place_ref[1] == 0)
        def _():
            state[layers + beyond :] = jnp.zeros((beyond, tiles, gz, LANES), f32)

    @pl.loop(0, layers + 4)
    def _(i):
        def emit(t, k, part, total):
            s1[i, t, part] = total

        apply(s0, i + 1, i, emit)

    clear(s1, 2)

    @pl.loop(0, layers + 2)
    def _(i):
        def emit(t, k, part, total):
            s2[i, t, part] = total - 24.5 * s0[i + 2, t, part]

        apply(s1, i + 1, i + 1, emit)

    clear(s2, 1)

    @pl.loop(0, layers)
    def _(i):
        held = {}

        def emit(t, k, part, total):
            held[k] = (total - 12.25 * s1[i + 2, t, part]) * (4.0 / 343.0)
            if k == 1:
                both = jnp.concatenate([held[0], held[1]], axis=0)
                out_ref[i, t * gz : (t + 1) * gz, :] = both.astype(bf16)

        apply(s2, i + 1, i + 2, emit)


def side_by_side(parts):
    return jnp.concatenate(parts, axis=1)


def gram_kernel(place_ref, own_ref, core_ref, half_ref, f_ref, part_ref, to_half):
    here, core = place_ref[2], place_ref[3]
    part = 0.0
    for (a, b), dual in zip(spots(here, core), (own_ref, core_ref, half_ref)):
        part = part + lax.dot_general(
            f_ref[2 * a + b], dual[...], (((0,), (0,)), ((), ())), preferred_element_type=f32
        )
    part_ref[...] = part
    first = 2 * (1 - here)
    to_half[...] = f_ref[pl.ds(first, 2)]


def last_gram_kernel(place_ref, both_ref, f_ref, part_ref, out_ref):
    pieces, height, _ = out_ref.shape
    a, b = spots(place_ref[2], place_ref[3])[3]
    part = part_ref[...] + lax.dot_general(
        f_ref[2 * a + b], both_ref[...], (((0,), (0,)), ((), ())), preferred_element_type=f32
    )
    out_ref[...] = part.T.astype(bf16).reshape(pieces, height, LANES)


def spots(here, core):
    return (here, core), (here, 1 - core), (1 - here, core), (1 - here, 1 - core)


def sum_kernel(in_ref, out_ref):
    count = in_ref.shape[0]
    total = in_ref[0].astype(f32)
    for k in range(1, count):
        total = total + in_ref[k].astype(f32)
    piece = total.astype(bf16)
    for k in range(out_ref.shape[0]):
        out_ref[k] = piece


def pick_kernel(place_ref, f_ref, half_ref, to_core):
    here, core = place_ref[2], place_ref[3]
    to_core[0] = f_ref[2 * here + 1 - core]
    to_core[1] = half_ref[1 - core]


def rows_of(g_ref, half, at):
    pieces, height, _ = g_ref.shape
    each = pieces // 2
    own = LANES // height
    return g_ref[pl.ds(half * each + at * own, own)].reshape(LANES, LANES)


def rotated_half(scale, place_ref, f_ref, half_ref, core_ref, g_ref):
    here, core = place_ref[2], place_ref[3]
    places = [
        2 * here + core,
        2 * (1 - here) + core,
        2 * here + 1 - core,
        2 * (1 - here) + 1 - core,
    ]
    cols = side_by_side([f_ref[places[0]], half_ref[core], core_ref[0], core_ref[1]])
    turn = side_by_side(
        [jnp.concatenate([rows_of(g_ref, k, at) for at in places], axis=0) for k in range(2)]
    )
    return (jnp.dot(cols, turn, preferred_element_type=f32) * scale).astype(bf16)


def rotate_half_kernel(scale, place_ref, f_ref, half_ref, core_ref, g_ref, out_ref):
    out_ref[...] = rotated_half(scale, place_ref, f_ref, half_ref, core_ref, g_ref)


def rotate_kernel(
    scale, place_ref, f_ref, half_ref, core_ref, g_ref, far_ref, done_ref, gram_ref, out_ref
):
    here, core = place_ref[2], place_ref[3]
    other = rotated_half(scale, place_ref, f_ref, half_ref, core_ref, far_ref)
    for k in range(2):
        cut = slice(k * LANES, (k + 1) * LANES)
        mine = pl.ds(pl.multiple_of((2 * k + core) * LANES, LANES), LANES)
        theirs = pl.ds(pl.multiple_of((2 * k + 1 - core) * LANES, LANES), LANES)
        out_ref[:, mine] = done_ref[:, cut]
        out_ref[:, theirs] = other[:, cut]
        at = 2 * here + core
        gram_ref[:, mine] = rows_of(g_ref, k, at).astype(f32)
        gram_ref[:, theirs] = rows_of(far_ref, k, at).astype(f32)


def shards(vectors, node_shift, coupling, dual_basis):
    layers, dofs, gy, gz, width = vectors.shape
    rows = dofs * gy * gz
    count = lax.axis_size(NODES)
    near = lax.axis_size(NEAR)
    far = lax.axis_size(FAR)
    blocks = lax.axis_size(COLS)
    cols = blocks * width
    height = cols // near
    v = vectors.reshape(layers, rows, width)

    def swap(array, axes):
        many = lax.axis_size(axes)
        return lax.ppermute(array, axes, [(i, many - 1 - i) for i in range(many)])

    def spread(array, axes):
        return lax.all_to_all(array, axes, split_axis=0, concat_axis=0, tiled=True)

    dual_half = swap(dual_basis, HALVES)
    dual_core = swap(dual_basis, "core")
    message = jax.ShapeDtypeStruct((REACH * rows + SHIFT_ROWS, width), bf16)
    up, down, shift_tile = pl.pallas_call(
        functools.partial(pack_kernel, rows),
        out_shape=(message, message, jax.ShapeDtypeStruct((SHIFT_ROWS, width), bf16)),
        in_specs=[pl.BlockSpec(memory_space=pltpu.HBM)] + vmem(1), out_specs=tuple(vmem(3)),
        scratch_shapes=[pltpu.VMEM((SHIFT_ROWS, width), f32), pltpu.SemaphoreType.DMA((2,))],
        compiler_params=room(8), name="pack",
    )(vectors.reshape(layers * rows, width), node_shift.transpose(1, 0, 2))
    low = lax.ppermute(up, NODES, [(i, i + 1) for i in range(count - 1)])
    high = lax.ppermute(down, NODES, [(i + 1, i) for i in range(count - 1)])
    dual_both = swap(dual_half, "core")
    node = lax.axis_index(NODES)
    place = jnp.stack(
        [node > 0, node < count - 1, lax.axis_index(HALVES), lax.axis_index("core")]
    ).astype(jnp.int32)
    tiles = dofs * gy
    own = pl.pallas_call(
        functools.partial(filter_kernel, gy, dofs),
        out_shape=jax.ShapeDtypeStruct((layers, rows, width), bf16),
        in_specs=smem(2) + vmem(4),
        out_specs=vmem(1)[0],
        scratch_shapes=[
            pltpu.VMEM((layers + 6, tiles, gz, width), f32),
            pltpu.VMEM((layers + 4, tiles, gz, width), f32),
            pltpu.VMEM((layers + 2, tiles, gz, width), f32),
            pltpu.VMEM((layers + 4, gy, gz, width), f32),
        ],
        compiler_params=room(16), name="filter",
    )(coupling, place, v, low, high, shift_tile)
    two = jax.ShapeDtypeStruct((2, rows, width), bf16)
    part, to_half = pl.pallas_call(
        gram_kernel,
        out_shape=(jax.ShapeDtypeStruct((width, cols), f32), two),
        in_specs=smem(1) + vmem(4), out_specs=tuple(vmem(2)), compiler_params=room(12),
        name="gram",
    )(place, dual_basis, dual_core, dual_half, own)
    terms = pl.pallas_call(
        last_gram_kernel,
        out_shape=jax.ShapeDtypeStruct((near, height, LANES), bf16),
        in_specs=smem(1) + vmem(3), out_specs=vmem(1)[0], compiler_params=room(12), name="last_gram",
    )(place, dual_both, own, part)
    from_half = swap(to_half, HALVES)
    pieces = spread(terms, NEAR)
    to_core = pl.pallas_call(
        pick_kernel,
        out_shape=two,
        in_specs=smem(1) + vmem(2), out_specs=vmem(1)[0], compiler_params=room(8), name="pick",
    )(place, own, from_half)
    from_core = swap(to_core, "core")

    def summed(pieces, copies):
        return pl.pallas_call(
            sum_kernel,
            out_shape=jax.ShapeDtypeStruct((copies, height, LANES), bf16),
            in_specs=vmem(1), out_specs=vmem(1)[0], compiler_params=room(8),
        )(pieces)

    pieces = spread(summed(pieces, far), FAR)
    pieces = spread(summed(pieces, 2 * near), (HALVES,) + NEAR)
    other = swap(pieces, "core")
    scale = cols ** (-0.5)
    half = pl.pallas_call(
        functools.partial(rotate_half_kernel, scale),
        out_shape=jax.ShapeDtypeStruct((rows, cols // 2), bf16),
        in_specs=smem(1) + vmem(4), out_specs=vmem(1)[0], compiler_params=room(8),
        name="rotate_half",
    )(place, own, from_half, from_core, pieces)
    gram, rotated = pl.pallas_call(
        functools.partial(rotate_kernel, scale),
        out_shape=(
            jax.ShapeDtypeStruct((cols // blocks, cols), f32),
            jax.ShapeDtypeStruct((rows, cols), bf16),
        ),
        in_specs=smem(1) + vmem(6), out_specs=tuple(vmem(2)), compiler_params=room(12), name="rotate",
    )(place, own, from_half, from_core, pieces, other, half)
    return gram, rotated


SIZES = (2, 4, 8, 2, 2, 2)


def solution(mesh):
    torus = Mesh(mesh.devices.reshape(SIZES), NODES + COLS)
    placed = (P(NODES, None, None, None, COLS), P(NODES, None, None), P(), P(NODES + COLS, None))
    return jax.shard_map(
        shards,
        mesh=torus,
        in_specs=placed,
        out_specs=(P(COLS, None), P(NODES + COLS, None)),
        check_vma=False,
    )
```

```python
import functools

import jax
import jax.numpy as jnp
from jax import lax
from jax.experimental import pallas as pl
from jax.experimental.pallas import tpu as pltpu
from jax.sharding import Mesh
from jax.sharding import PartitionSpec as P


NODES = ("x_lo", "y", "z_hi", "z_lo")
COLS = ("x_hi", "core")
NEAR = ("x_lo", "y", "z_lo")
HALVES = "x_hi"
FAR = "z_hi"
REACH = 3
TILE_ROWS = 16
LANES = 128
SHIFT_ROWS = 32

bf16 = jnp.bfloat16
f32 = jnp.float32


def vmem(count):
    return [pl.BlockSpec(memory_space=pltpu.VMEM)] * count


def smem(count):
    return [pl.BlockSpec(memory_space=pltpu.SMEM)] * count


def room(mebibytes):
    return pltpu.CompilerParams(vmem_limit_bytes=mebibytes << 20)


def pack_kernel(rows, v_ref, shift_ref, up_ref, down_ref, tile_ref, spread, sems):
    span = REACH * rows
    total = v_ref.shape[0]
    copies = [
        pltpu.make_async_copy(v_ref.at[total - span : total], up_ref.at[0:span], sems.at[0]),
        pltpu.make_async_copy(v_ref.at[0:span], down_ref.at[0:span], sems.at[1]),
    ]
    for copy in copies:
        copy.start()
    gy, layers, gz = shift_ref.shape
    spread[...] = jnp.zeros_like(spread)
    for y in range(gy):
        spread[y * layers : (y + 1) * layers, 0:gz] = shift_ref[y].astype(f32)
    tile = spread[...].astype(bf16)
    tile_ref[...] = tile
    up_ref[span:, :] = tile
    down_ref[span:, :] = tile
    for copy in copies:
        copy.wait()


def filter_kernel(
    gy, dofs, coup_ref, place_ref, v_ref, low_ref, high_ref, shift_ref, out_ref, s0, s1, s2, diag
):
    layers = v_ref.shape[0]
    gz = TILE_ROWS
    half = gz // 2
    rows = dofs * gy * gz
    tiles = dofs * gy
    span = REACH * rows

    stiff = jnp.concatenate(
        [low_ref[span:, :], shift_ref[...], high_ref[span:, :]]
        + [jnp.zeros((LANES - 3 * SHIFT_ROWS, LANES), bf16)],
        axis=0,
    )
    stiff = stiff.astype(f32).T
    firsts = [layers - 2 + k for k in range(2)]
    firsts += [SHIFT_ROWS + k for k in range(layers)]
    firsts += [2 * SHIFT_ROWS + k for k in range(2)]
    for slot, first in enumerate(firsts):
        for y in range(gy):
            lane = first + y * layers
            column = stiff[0:gz, lane : lane + 1]
            diag[slot, y] = jnp.broadcast_to(column, (gz, LANES)) - 4.0

    for t in range(tiles):
        for k in range(REACH):
            at = k * rows + t * gz
            s0[k, t] = low_ref[at : at + gz, :].astype(f32)
            s0[REACH + layers + k, t] = high_ref[at : at + gz, :].astype(f32)
        for k in range(layers):
            s0[REACH + k, t] = v_ref[k, t * gz : (t + 1) * gz, :].astype(f32)

    row = lax.broadcasted_iota(jnp.int32, (half, LANES), 0)
    top, bottom = row == 0, row == half - 1
    coup = [[coup_ref[d, e] for e in range(dofs)] for d in range(dofs)]
    halves = (slice(0, half), slice(half, gz))

    def apply(src, at, dslot, emit):
        for y in range(gy):
            mid = [[src[at, d * gy + y, part] for part in halves] for d in range(dofs)]
            dg = [diag[dslot, y, part] for part in halves]
            for d in range(dofs):
                t = d * gy + y
                up = [pltpu.roll(mid[d][k], 1, 0) for k in range(2)]
                down = [pltpu.roll(mid[d][k], half - 1, 0) for k in range(2)]
                shifted = (
                    jnp.where(top, 0.0, up[0]) + jnp.where(bottom, down[1], down[0]),
                    jnp.where(top, up[0], up[1]) + jnp.where(bottom, 0.0, down[1]),
                )
                for k, part in enumerate(halves):
                    near = src[at - 1, t, part] + src[at + 1, t, part]
                    if y > 0:
                        near = near + src[at, t - 1, part]
                    if y < gy - 1:
                        near = near + src[at, t + 1, part]
                    near = near + shifted[k]
                    total = (dg[k] + coup[d][d]) * mid[d][k] - near
                    for e in range(dofs):
                        if e != d:
                            total = total + coup[d][e] * mid[e][k]
                    emit(t, k, part, total)

    def clear(state, beyond):
        @pl.when(place_ref[0] == 0)
        def _():
            state[0:beyond] = jnp.zeros((beyond, tiles, gz, LANES), f32)

        @pl.when(place_ref[1] == 0)
        def _():
            state[layers + beyond :] = jnp.zeros((beyond, tiles, gz, LANES), f32)

    @pl.loop(0, layers + 4)
    def _(i):
        def emit(t, k, part, total):
            s1[i, t, part] = total

        apply(s0, i + 1, i, emit)

    clear(s1, 2)

    @pl.loop(0, layers + 2)
    def _(i):
        def emit(t, k, part, total):
            s2[i, t, part] = total - 24.5 * s0[i + 2, t, part]

        apply(s1, i + 1, i + 1, emit)

    clear(s2, 1)

    @pl.loop(0, layers)
    def _(i):
        held = {}

        def emit(t, k, part, total):
            held[k] = (total - 12.25 * s1[i + 2, t, part]) * (4.0 / 343.0)
            if k == 1:
                both = jnp.concatenate([held[0], held[1]], axis=0)
                out_ref[i, t * gz : (t + 1) * gz, :] = both.astype(bf16)

        apply(s2, i + 1, i + 2, emit)


def side_by_side(parts):
    return jnp.concatenate(parts, axis=1)


def gram_kernel(
    place_ref, own_ref, core_ref, half_ref, both_ref, f_ref, out_ref, to_half
):
    pieces, height, _ = out_ref.shape
    here, core = place_ref[2], place_ref[3]
    layers = [2 * a + b for a, b in spots(here, core)]
    part = 0.0
    for at, dual in zip(layers, (own_ref, core_ref, half_ref, both_ref)):
        part = part + lax.dot_general(
            f_ref[at], dual[...], (((0,), (0,)), ((), ())), preferred_element_type=f32
        )
    out_ref[...] = part.T.astype(bf16).reshape(pieces, height, LANES)
    first = 2 * (1 - here)
    to_half[...] = f_ref[pl.ds(first, 2)]


def spots(here, core):
    return (here, core), (here, 1 - core), (1 - here, core), (1 - here, 1 - core)


def sum_kernel(in_ref, out_ref):
    count = in_ref.shape[0]
    total = in_ref[0].astype(f32)
    for k in range(1, count):
        total = total + in_ref[k].astype(f32)
    piece = total.astype(bf16)
    for k in range(out_ref.shape[0]):
        out_ref[k] = piece


def pick_kernel(place_ref, f_ref, half_ref, to_core):
    here, core = place_ref[2], place_ref[3]
    to_core[0] = f_ref[2 * here + 1 - core]
    to_core[1] = half_ref[1 - core]


def rows_of(g_ref, half, at):
    pieces, height, _ = g_ref.shape
    each = pieces // 2
    own = LANES // height
    return g_ref[pl.ds(half * each + at * own, own)].reshape(LANES, LANES)


def rotated_half(scale, place_ref, f_ref, half_ref, core_ref, g_ref):
    here, core = place_ref[2], place_ref[3]
    places = [
        2 * here + core,
        2 * (1 - here) + core,
        2 * here + 1 - core,
        2 * (1 - here) + 1 - core,
    ]
    cols = side_by_side([f_ref[places[0]], half_ref[core], core_ref[0], core_ref[1]])
    turn = side_by_side(
        [jnp.concatenate([rows_of(g_ref, k, at) for at in places], axis=0) for k in range(2)]
    )
    return (jnp.dot(cols, turn, preferred_element_type=f32) * scale).astype(bf16)


def rotate_half_kernel(scale, place_ref, f_ref, half_ref, core_ref, g_ref, out_ref):
    out_ref[...] = rotated_half(scale, place_ref, f_ref, half_ref, core_ref, g_ref)


def rotate_kernel(
    scale, place_ref, f_ref, half_ref, core_ref, g_ref, far_ref, done_ref, gram_ref, out_ref
):
    here, core = place_ref[2], place_ref[3]
    other = rotated_half(scale, place_ref, f_ref, half_ref, core_ref, far_ref)
    for k in range(2):
        cut = slice(k * LANES, (k + 1) * LANES)
        mine = pl.ds(pl.multiple_of((2 * k + core) * LANES, LANES), LANES)
        theirs = pl.ds(pl.multiple_of((2 * k + 1 - core) * LANES, LANES), LANES)
        out_ref[:, mine] = done_ref[:, cut]
        out_ref[:, theirs] = other[:, cut]
        at = 2 * here + core
        gram_ref[:, mine] = rows_of(g_ref, k, at).astype(f32)
        gram_ref[:, theirs] = rows_of(far_ref, k, at).astype(f32)


def shards(vectors, node_shift, coupling, dual_basis):
    layers, dofs, gy, gz, width = vectors.shape
    rows = dofs * gy * gz
    count = lax.axis_size(NODES)
    near = lax.axis_size(NEAR)
    far = lax.axis_size(FAR)
    blocks = lax.axis_size(COLS)
    cols = blocks * width
    height = cols // near
    v = vectors.reshape(layers, rows, width)

    def swap(array, axes):
        many = lax.axis_size(axes)
        return lax.ppermute(array, axes, [(i, many - 1 - i) for i in range(many)])

    def spread(array, axes):
        return lax.all_to_all(array, axes, split_axis=0, concat_axis=0, tiled=True)

    dual_half = swap(dual_basis, HALVES)
    dual_core = swap(dual_basis, "core")
    message = jax.ShapeDtypeStruct((REACH * rows + SHIFT_ROWS, width), bf16)
    up, down, shift_tile = pl.pallas_call(
        functools.partial(pack_kernel, rows),
        out_shape=(message, message, jax.ShapeDtypeStruct((SHIFT_ROWS, width), bf16)),
        in_specs=[pl.BlockSpec(memory_space=pltpu.HBM)] + vmem(1), out_specs=tuple(vmem(3)),
        scratch_shapes=[pltpu.VMEM((SHIFT_ROWS, width), f32), pltpu.SemaphoreType.DMA((2,))],
        compiler_params=room(60), name="pack",
    )(vectors.reshape(layers * rows, width), node_shift.transpose(1, 0, 2))
    low = lax.ppermute(up, NODES, [(i, i + 1) for i in range(count - 1)])
    high = lax.ppermute(down, NODES, [(i + 1, i) for i in range(count - 1)])
    dual_both = swap(dual_half, "core")
    node = lax.axis_index(NODES)
    place = jnp.stack(
        [node > 0, node < count - 1, lax.axis_index(HALVES), lax.axis_index("core")]
    ).astype(jnp.int32)
    tiles = dofs * gy
    own = pl.pallas_call(
        functools.partial(filter_kernel, gy, dofs),
        out_shape=jax.ShapeDtypeStruct((layers, rows, width), bf16),
        in_specs=smem(2) + vmem(4),
        out_specs=vmem(1)[0],
        scratch_shapes=[
            pltpu.VMEM((layers + 6, tiles, gz, width), f32),
            pltpu.VMEM((layers + 4, tiles, gz, width), f32),
            pltpu.VMEM((layers + 2, tiles, gz, width), f32),
            pltpu.VMEM((layers + 4, gy, gz, width), f32),
        ],
        compiler_params=room(16), name="filter",
    )(coupling, place, v, low, high, shift_tile)
    two = jax.ShapeDtypeStruct((2, rows, width), bf16)
    terms, to_half = pl.pallas_call(
        gram_kernel,
        out_shape=(jax.ShapeDtypeStruct((near, height, LANES), bf16), two),
        in_specs=smem(1) + vmem(5), out_specs=tuple(vmem(2)), compiler_params=room(12), name="gram",
    )(place, dual_basis, dual_core, dual_half, dual_both, own)
    from_half = swap(to_half, HALVES)
    pieces = spread(terms, NEAR)
    to_core = pl.pallas_call(
        pick_kernel,
        out_shape=two,
        in_specs=smem(1) + vmem(2), out_specs=vmem(1)[0], compiler_params=room(8), name="pick",
    )(place, own, from_half)
    from_core = swap(to_core, "core")

    def summed(pieces, copies):
        return pl.pallas_call(
            sum_kernel,
            out_shape=jax.ShapeDtypeStruct((copies, height, LANES), bf16),
            in_specs=vmem(1), out_specs=vmem(1)[0], compiler_params=room(8),
        )(pieces)

    pieces = spread(summed(pieces, far), FAR)
    pieces = spread(summed(pieces, 2 * near), (HALVES,) + NEAR)
    other = swap(pieces, "core")
    scale = cols ** (-0.5)
    half = pl.pallas_call(
        functools.partial(rotate_half_kernel, scale),
        out_shape=jax.ShapeDtypeStruct((rows, cols // 2), bf16),
        in_specs=smem(1) + vmem(4), out_specs=vmem(1)[0], compiler_params=room(8),
        name="rotate_half",
    )(place, own, from_half, from_core, pieces)
    gram, rotated = pl.pallas_call(
        functools.partial(rotate_kernel, scale),
        out_shape=(
            jax.ShapeDtypeStruct((cols // blocks, cols), f32),
            jax.ShapeDtypeStruct((rows, cols), bf16),
        ),
        in_specs=smem(1) + vmem(6), out_specs=tuple(vmem(2)), compiler_params=room(12), name="rotate",
    )(place, own, from_half, from_core, pieces, other, half)
    return gram, rotated


SIZES = (2, 4, 8, 2, 2, 2)


def solution(mesh):
    torus = Mesh(mesh.devices.reshape(SIZES), NODES + COLS)
    placed = (P(NODES, None, None, None, COLS), P(NODES, None, None), P(), P(NODES + COLS, None))
    return jax.shard_map(
        shards,
        mesh=torus,
        in_specs=placed,
        out_specs=(P(COLS, None), P(NODES + COLS, None)),
        check_vma=False,
    )
```
